128 devices in a mesh: layer: 32 (over x, z, core), batch: 4 (over y).
Axes of the slice: x: 4, y: 4, z: 4, core: 2. Of those that a mesh axis runs over, the one named last changes fastest.
Arguments:
- first_state: float32 [4, 32, 32, 256], P('batch'), may hold values from -6 to 6
- guess_points: float32 [32, 4, 32, 32, 256], P('layer', 'batch'), may hold values from -6 to 6
- weights: bfloat16 [128, 3, 3, 256, 256], P('layer'), may hold values from -0.5 to 0.5
Outputs:
- states: float32 [128, 4, 32, 32, 256], P('layer', 'batch')
- norms: float32 [32], P('layer')
The draws below stay inside these ranges and needn't reach their ends.
All inputs are finite; a program needn't handle non-finite values.
Results may differ from the reference program's by a relative error of at most 0.0038.
Values sent between devices are 32-bit elements; how exact they have to be, the bound alone decides.
No kernel may reach another device: no remote copies, remote signals or barrier semaphores. Data moves between devices by JAX's collectives and lax.ppermute only.
A program may use at most 128 MiB of HBM per device.

```python
import jax
import jax.numpy as jnp
from jax import lax

CH = 256
IMG = 32
BLOCK = 4
BLOCKS = 32
GROUPS = 8
LAYERS = 128
BATCH = 4


def levels(stream_key, extent, pieces, least, top_value):
    loudness, own = 1.0, jax.random.fold_in(stream_key, 6)
    for position, parts in pieces:
        heights = jnp.exp(jax.random.uniform(jax.random.fold_in(own, position), (parts,), jnp.float32, least / len(pieces), top_value / len(pieces)))
        loudness = loudness * jnp.repeat(heights, extent[position] // parts).reshape([-1 if axis == position else 1 for axis in range(len(extent))])
    return loudness


def scatter_about(stream_key, shape, width, bound, pieces=(), kind=jnp.bfloat16):
    result = jax.random.normal(stream_key, shape, jnp.float32) * width
    if len(pieces) > 0:
        result = levels(stream_key, shape, pieces, -0.22, 0.18) * result
    return jnp.clip(result, min=-bound, max=bound).astype(kind)


def setup_inputs(seed: int = 0) -> dict:
    key_list = jax.random.split(jax.random.key(seed), 4)
    return {
        "first_state": scatter_about(key_list[0], (BATCH, IMG, IMG, CH), 1.0, 6.0, ((0, 4),), jnp.float32),
        "guess_points": scatter_about(key_list[1], (BLOCKS, BATCH, IMG, IMG, CH), 1.0, 6.0, ((0, 32), (1, 4)), jnp.float32),
        "weights": scatter_about(key_list[2], (LAYERS, 3, 3, CH, CH), (9 * CH // 16) ** -0.5, 0.5, ((0, 32),)),
    }


def propagate(state, weight, factor):
    mixed = lax.conv_general_dilated(state.astype(jnp.bfloat16), weight, (1, 1), 'SAME', dimension_numbers=('NHWC', 'HWIO', 'NHWC'), preferred_element_type=jnp.float32)
    return state + factor * jax.nn.relu(mixed)

def shifted(first_state, stacked):
    return jnp.concatenate([first_state[None], stacked[:-1]], axis=0)

def reference(first_state, guess_points, weights):
    vstep = jax.vmap(propagate, in_axes=(0, 0, None))
    step_size = 2.0 / LAYERS
    blocked = weights.reshape(BLOCKS, BLOCK, 3, 3, CH, CH)

    def block_sweep(state):
        for slot in range(BLOCK):
            state = vstep(state, blocked[:, slot], step_size)
        return state
    relaxed = block_sweep(shifted(first_state, guess_points))
    entry_state = shifted(first_state, relaxed)
    swept = block_sweep(entry_state)
    residual = swept - relaxed
    norms = jnp.sqrt(lax.optimization_barrier(jnp.sum(residual * residual, axis=(1, 2, 3, 4))) / (BATCH * IMG * IMG * CH) + 1e-06)
    fine_rhs = swept - vstep(entry_state, blocked[:, 0], 4.0 * step_size)
    group_weights = blocked[:, 0].reshape(GROUPS, BLOCK, 3, 3, CH, CH)
    group_rhs_fine = fine_rhs.reshape(GROUPS, BLOCK, BATCH, IMG, IMG, CH)

    def group_sweep(state, length):
        results = []
        for slot in range(length):
            state = vstep(state, group_weights[:, slot], 4.0 * step_size) + group_rhs_fine[:, slot]
            results.append(state)
        return results
    group_entry = shifted(first_state, relaxed[BLOCK - 1::BLOCK])
    group_ends = group_sweep(group_entry, BLOCK)[-1]
    previous_ends = shifted(first_state, group_ends)
    group_rhs = group_sweep(previous_ends, BLOCK)[-1] - vstep(previous_ends, group_weights[:, 0], 16.0 * step_size)
    coarse_state = first_state
    coarse_list = []
    for group in range(GROUPS):
        coarse_state = propagate(coarse_state, group_weights[group, 0], 16.0 * step_size) + group_rhs[group]
        coarse_list.append(coarse_state)
    coarse_states = jnp.stack(coarse_list)
    corrected = group_sweep(shifted(first_state, coarse_states), BLOCK - 1)
    corrected.append(coarse_states)
    coarse_final = jnp.stack(corrected, axis=1).reshape(BLOCKS, BATCH, IMG, IMG, CH)
    moving = shifted(first_state, coarse_final)
    results = []
    for slot in range(BLOCK - 1):
        moving = vstep(moving, blocked[:, slot], step_size)
        results.append(moving)
    results.append(coarse_final)
    states = jnp.stack(results, axis=1).reshape(LAYERS, BATCH, IMG, IMG, CH)
    return (states, norms)
```

```python
import functools

import jax
import jax.numpy as jnp
from jax import lax
from jax.experimental import pallas as pl
from jax.experimental.pallas import tpu as pltpu
from jax.sharding import PartitionSpec as P


CH = 256
SIDE = 32
ROWS = SIDE * SIDE
TAPS = 9 * CH
TILE = 256
H = 2.0 / 128
STATE = jax.ShapeDtypeStruct((ROWS, CH), jnp.float32)
ANY = pl.BlockSpec(memory_space=pl.ANY)
VMEM = pl.BlockSpec(memory_space=pltpu.VMEM)


def stencil_put(buf, r, value):
    rows = value.shape[0]
    column = lax.broadcasted_iota(jnp.int32, (rows, CH), 0) % SIDE
    before = jnp.where(column == 0, 0.0, pltpu.roll(value, 1, 0))
    behind = jnp.where(column == SIDE - 1, 0.0, pltpu.roll(value, rows - 1, 0))
    at = pl.ds(SIDE + r, rows)
    buf[at, 0:CH] = before.astype(jnp.bfloat16)
    buf[at, CH : 2 * CH] = value.astype(jnp.bfloat16)
    buf[at, 2 * CH : 3 * CH] = behind.astype(jnp.bfloat16)


def stencil_pads(*bufs):
    zero = jnp.zeros((SIDE, 3 * CH), jnp.bfloat16)
    for buf in bufs:
        buf[0:SIDE, :] = zero
        buf[SIDE + ROWS :, :] = zero


def relu_conv(buf, weight, r):
    total = None
    for dy in range(3):
        part = jnp.dot(
            buf[pl.ds(r + SIDE * dy, TILE), :],
            weight[pl.ds(3 * CH * dy, 3 * CH), :],
            preferred_element_type=jnp.float32,
        )
        total = part if total is None else total + part
    return jnp.maximum(total, 0.0)


def run_steps(start, bufs, held, steps):
    for r in range(0, ROWS, TILE):
        stencil_put(bufs[0], r, start[r : r + TILE, :])
    for n, (ready, weight, update) in enumerate(steps):
        ready()
        source, target = bufs[n % 2], bufs[(n + 1) % 2]
        current = start if n == 0 else held
        for r in range(0, ROWS, TILE):
            value = update(r, current[r : r + TILE, :], relu_conv(source, weight, r))
            if n + 1 < len(steps):
                held[r : r + TILE, :] = value
                stencil_put(target, r, value)


SCRATCH = (
    pltpu.VMEM((ROWS + 2 * SIDE, 3 * CH), jnp.bfloat16),
    pltpu.VMEM((ROWS + 2 * SIDE, 3 * CH), jnp.bfloat16),
    pltpu.VMEM((ROWS, CH), jnp.float32),
)


def pick(choices, target, sem):
    for condition, source in choices:

        @pl.when(condition)
        def _(source=source):
            pltpu.make_async_copy(source, target, sem).start()

    return lambda: pltpu.make_async_copy(choices[0][1], target, sem).wait()


def fetch(source, target, sem):
    copy = pltpu.make_async_copy(source, target, sem)
    copy.start()
    return copy.wait


def spot():
    d = lax.axis_index("layer")
    return d, d // 8, (d // 2) % 4, d % 2


def nothing():
    return None


def kernel_call(body, outs, out_specs, args, in_specs, scratch, convs, name, aliases=None):
    return pl.pallas_call(
        body,
        out_shape=outs,
        in_specs=in_specs,
        out_specs=out_specs,
        scratch_shapes=scratch,
        input_output_aliases=aliases or {},
        compiler_params=pltpu.CompilerParams(vmem_limit_bytes=48 << 20),
        cost_estimate=pl.CostEstimate(
            flops=convs * 2 * ROWS * TAPS * CH, bytes_accessed=4 << 20, transcendentals=0
        ),
        name=name,
    )(*args)


def wbuf(n):
    return [pltpu.VMEM((n, TAPS, CH), jnp.bfloat16), pltpu.SemaphoreType.DMA((n,))]


def sweep_body(first, given, w, out, b0, b1, held, x, xs, wv, ws):
    d = lax.axis_index("layer")
    got = pick([(d == 0, first), (d != 0, given)], x, xs)
    waits = [fetch(w.at[n], wv.at[n], ws.at[n]) for n in range(4)]
    stencil_pads(b0, b1)
    got()

    def layer(r, v, a):
        return v + H * a

    def last(r, v, a):
        out[r : r + TILE, :] = v + H * a

    run_steps(x, (b0, b1), held, [(waits[n], wv.at[n], layer if n < 3 else last) for n in range(4)])


def sweep(first, given, w):
    return kernel_call(
        sweep_body, STATE, VMEM, (first, given, w), [ANY] * 3,
        [*SCRATCH, pltpu.VMEM((ROWS, CH), jnp.float32), pltpu.SemaphoreType.DMA, *wbuf(4)], 4, "sweep",
    )


def resweep_body(first, given, w, relaxed, fine, send, squares, b0, b1, held, x, xs, wv, ws, ahead):
    d = lax.axis_index("layer")
    got = pick([(d == 0, first), (d != 0, given)], x, xs)
    waits = [fetch(w.at[n], wv.at[n], ws.at[n]) for n in range(4)]
    stencil_pads(b0, b1)
    squares[...] = jnp.zeros_like(squares)
    got()

    def head(r, v, a):
        ahead[r : r + TILE, :] = v + 4 * H * a
        return v + H * a

    def layer(r, v, a):
        return v + H * a

    def last(r, v, a):
        value = v + H * a
        rhs = value - ahead[r : r + TILE, :]
        fine[r : r + TILE, :] = rhs
        off = value - relaxed[r : r + TILE, :]
        squares[...] += jnp.sum((off * off).reshape(TILE // 8, 8, CH), axis=0)
        send[r : r + TILE, :] = jnp.where(d % 4 < 2, value, rhs)

    run_steps(x, (b0, b1), held, [(waits[n], wv.at[n], (head, layer, layer, last)[n]) for n in range(4)])


def resweep(first, given, w, relaxed):
    return kernel_call(
        resweep_body, (STATE, STATE, jax.ShapeDtypeStruct((8, CH), jnp.float32)), (VMEM,) * 3,
        (first, given, w, relaxed), [ANY, ANY, ANY, VMEM],
        [*SCRATCH, pltpu.VMEM((ROWS, CH), jnp.float32), pltpu.SemaphoreType.DMA, *wbuf(4),
         pltpu.VMEM((ROWS, CH), jnp.float32)], 4, "resweep",
    )


def coarse_update(rhs):
    return lambda r, v, a: v + 4 * H * a + rhs[r : r + TILE, :]


def coarse_last(rhs, out):
    def update(r, v, a):
        out[r : r + TILE, :] = v + 4 * H * a + rhs[r : r + TILE, :]

    return update


def one_coarse_body(x, w, rhs, out, b0, b1, held, wv, ws):
    wait = fetch(w.at[0], wv.at[0], ws.at[0])
    stencil_pads(b0, b1)
    run_steps(x, (b0, b1), held, [(wait, wv.at[0], coarse_last(rhs, out))])


def one_coarse(x, w, rhs):
    return kernel_call(
        one_coarse_body, STATE, VMEM, (x, w, rhs), [VMEM, ANY, VMEM], [*SCRATCH, *wbuf(1)], 1, "one_coarse"
    )


def two_coarse_body(x, wa, w, rhs_a, rhs_b, out, b0, b1, held, wv, ws):
    waits = [fetch(wa, wv.at[0], ws.at[0]), fetch(w.at[0], wv.at[1], ws.at[1])]
    stencil_pads(b0, b1)
    run_steps(
        x, (b0, b1), held,
        [(waits[0], wv.at[0], coarse_update(rhs_a)), (waits[1], wv.at[1], coarse_last(rhs_b, out))],
    )


def two_coarse(x, wa, w, rhs_a, rhs_b):
    return kernel_call(
        two_coarse_body, STATE, VMEM, (x, wa, w, rhs_a, rhs_b), [VMEM, ANY, ANY, VMEM, VMEM],
        [*SCRATCH, *wbuf(2)], 2, "two_coarse",
    )


def group_body(first, ends, w0, w1, w2, w3, f0, f1, f2, f3, out, b0, b1, held, x, xs, wv, ws, ahead):
    d = lax.axis_index("layer")
    got = pick([(d == 1, first), (d != 1, ends)], x, xs)
    waits = [fetch(s, wv.at[n], ws.at[n]) for n, s in enumerate((w0, w1.at[0], w2, w3))]
    stencil_pads(b0, b1)
    got()

    def head(r, v, a):
        ahead[r : r + TILE, :] = v + 16 * H * a
        return v + 4 * H * a + f0[r : r + TILE, :]

    def last(r, v, a):
        value = v + 4 * H * a + f3[r : r + TILE, :]
        out[r : r + TILE, :] = jnp.where(d == 5, value, value - ahead[r : r + TILE, :])

    updates = (head, coarse_update(f1), coarse_update(f2), last)
    run_steps(x, (b0, b1), held, [(waits[n], wv.at[n], updates[n]) for n in range(4)])


def group(*args):
    return kernel_call(
        group_body, STATE, VMEM, args, [ANY] * 6 + [VMEM] * 4,
        [*SCRATCH, pltpu.VMEM((ROWS, CH), jnp.float32), pltpu.SemaphoreType.DMA, *wbuf(4),
         pltpu.VMEM((ROWS, CH), jnp.float32)], 4, "group",
    )


def relay_body(came2, came3, rhs2, rhs3, we2, we3, w02, w03, own2, own3, ca, cb,
               b0, b1, held, x, ra, rb, xs, wv, ws):
    _, _, z, _ = spot()
    third = z == 3
    other = z != 3
    got = pick([(third, came3), (other, came2)], x, xs.at[0])
    got_w = [pick([(third, we3), (other, we2)], wv.at[0], ws.at[0]),
             pick([(third, w03), (other, w02)], wv.at[1], ws.at[1])]
    got_a = pick([(third, rhs3), (other, rhs2)], ra, xs.at[1])
    got_b = pick([(third, own3), (other, own2)], rb, xs.at[2])
    stencil_pads(b0, b1)
    got()
    got_a()
    got_b()

    def first(r, v, a):
        value = v + 16 * H * a + ra[r : r + TILE, :]
        ca[r : r + TILE, :] = value
        return value

    def second(r, v, a):
        cb[r : r + TILE, :] = v + 16 * H * a + rb[r : r + TILE, :]

    run_steps(x, (b0, b1), held, [(got_w[0], wv.at[0], first), (got_w[1], wv.at[1], second)])


def relay(*args):
    return kernel_call(
        relay_body, (STATE, STATE), (VMEM, VMEM), args, [ANY] * 10,
        [*SCRATCH, *[pltpu.VMEM((ROWS, CH), jnp.float32)] * 3, pltpu.SemaphoreType.DMA((3,)), *wbuf(2)], 2, "relay",
    )


def choose_body(ends, made, got, cb1, cb2, out, sem):
    _, x, z, _ = spot()
    pick([((x == 0) & (z < 2), ends), ((x == 0) & (z == 2), made), ((x == 0) & (z == 3), got),
          (x == 1, cb1), (x >= 2, cb2)], out, sem)()


def choose(*args):
    return kernel_call(choose_body, STATE, VMEM, args, [ANY] * 5, [pltpu.SemaphoreType.DMA], 0, "choose")


def correct_body(first, ends_in, even_in, ca1, ca2, came, rhs2, rhs3, we2, we3, wa0, wb0, wa1, wb1,
                 fa0, fb0, fa1, fb1, made, got, ends, send, move, coarse,
                 b0, b1, held, x, ra, g0, g1, rk, xs, wv, ws):
    d, xc, z, _ = spot()
    is_a = z % 2 == 0
    is_b = z % 2 == 1
    odd = z >= 2
    third = z == 3
    late = (xc == 3) & odd
    got_x = pick(
        [((xc == 0) & (z < 2), first), ((xc == 0) & (z == 2), ends_in),
         (((xc == 0) & third) | ((xc > 0) & (z < 2)), even_in),
         ((xc == 1) & odd, ca1), ((xc == 2) & odd, ca2), (late, came)], x, xs.at[0])
    got_w = [pick([(third, we3), (jnp.logical_not(third), we2)], wv.at[0], ws.at[0]),
             pick([(is_a, wa0), (is_b, wb0)], wv.at[1], ws.at[1]),
             pick([(is_a, wa1.at[0]), (is_b, wb1)], wv.at[2], ws.at[2])]
    got_ra = pick([(third, rhs3), (jnp.logical_not(third), rhs2)], ra, xs.at[1])
    got_f = [pick([(is_a, fa0), (is_b, fb0)], g0, xs.at[2]), pick([(is_a, fa1), (is_b, fb1)], g1, xs.at[3])]
    got_r = pick([(is_a, made), (is_b & (d // 4 > 0), got), (is_b & (d // 4 == 0), ends)], rk, xs.at[4])
    stencil_pads(b0, b1)
    got_x()
    got_w[0]()
    got_ra()

    @pl.when(late)
    def _():
        def update(r, v, a):
            held[r : r + TILE, :] = v + 16 * H * a + ra[r : r + TILE, :]

        run_steps(x, (b0, b1), held, [(nothing, wv.at[0], update)])
        x[...] = held[...]

    for wait in (*got_f, got_r):
        wait()

    def zero(r, v, a):
        rk_rows = rk[r : r + TILE, :]
        coarse[r : r + TILE, :] = jnp.where(d // 4 < 2, rk_rows, v + 16 * H * a + rk_rows)
        value = v + 4 * H * a + g0[r : r + TILE, :]
        move[r : r + TILE, :] = value
        send[r : r + TILE, :] = v
        return value

    def one(r, v, a):
        @pl.when(is_b)
        def _():
            value = v + 4 * H * a + g1[r : r + TILE, :]
            move[r : r + TILE, :] = value
            send[r : r + TILE, :] = value

    run_steps(x, (b0, b1), held, [(got_w[1], wv.at[1], zero), (got_w[2], wv.at[2], one)])


def correct(*args):
    return kernel_call(
        correct_body, (STATE,) * 3, (VMEM,) * 3, args, [ANY] * 21,
        [*SCRATCH, *[pltpu.VMEM((ROWS, CH), jnp.float32)] * 5, pltpu.SemaphoreType.DMA((5,)), *wbuf(3)], 3, "correct",
    )


def finish(x, w, rhs, start_step, out, stage, os, bufs, held, wv, waits, last_state):
    copies = [pltpu.make_async_copy(stage.at[n], out.at[n], os.at[n]) for n in range(4)]

    def layer(n):
        def update(r, v, a):
            value = v + H * a
            stage[n, r : r + TILE, :] = value
            if n == 0:
                coarse = v + 4 * H * a + rhs[r : r + TILE, :]
                stage[3, r : r + TILE, :] = coarse if last_state is None else last_state(r, coarse)
            if r + TILE == ROWS:
                copies[n].start()
                if n == 0:
                    copies[3].start()
            return value

        return update

    run_steps(x, bufs, held, start_step + [(waits[n], wv.at[n], layer(n)) for n in range(3)])
    for copy in copies:
        copy.wait()


def finish_one_body(x, coarse, w, w2, f2, rhs, out, b0, b1, held, xb, wv, ws, w2v, stage, os):
    _, _, z, core = spot()

    @pl.when(core == 1)
    def _():
        waits = [fetch(w.at[n], wv.at[n], ws.at[n]) for n in range(3)]
        got_w2 = fetch(w2, w2v, ws.at[3])
        stencil_pads(b0, b1)
        got_w2()
        xb[...] = x[...]

        @pl.when(z % 2 == 1)
        def _():
            def update(r, v, a):
                xb[r : r + TILE, :] = v + 4 * H * a + f2[r : r + TILE, :]

            run_steps(x, (b0, b1), held, [(nothing, w2v, update)])

        def last_state(r, value):
            return jnp.where(z % 2 == 1, coarse[r : r + TILE, :], value)

        finish(xb, w, rhs, [], out, stage, os, (b0, b1), held, wv, waits, last_state)


OUT = jax.ShapeDtypeStruct((4, ROWS, CH), jnp.float32)


def finish_one(x, coarse, w, w2, f2, rhs):
    return kernel_call(
        finish_one_body, OUT, ANY, (x, coarse, w, w2, f2, rhs), [VMEM, VMEM, ANY, ANY, VMEM, VMEM],
        [*SCRATCH, pltpu.VMEM((ROWS, CH), jnp.float32), pltpu.VMEM((3, TAPS, CH), jnp.bfloat16),
         pltpu.SemaphoreType.DMA((4,)), pltpu.VMEM((TAPS, CH), jnp.bfloat16),
         pltpu.VMEM((4, ROWS, CH), jnp.float32), pltpu.SemaphoreType.DMA((4,))], 4, "finish_one",
    )


def finish_zero_body(x, w, rhs, so_far, out, b0, b1, held, wv, ws, stage, os):
    _, _, _, core = spot()

    @pl.when(core == 0)
    def _():
        waits = [fetch(w.at[n], wv.at[n], ws.at[n]) for n in range(3)]
        stencil_pads(b0, b1)
        finish(x, w, rhs, [], out, stage, os, (b0, b1), held, wv, waits, None)


def finish_zero(x, w, rhs, so_far):
    return kernel_call(
        finish_zero_body, OUT, ANY, (x, w, rhs, so_far), [VMEM, ANY, VMEM, ANY],
        [*SCRATCH, pltpu.VMEM((3, TAPS, CH), jnp.bfloat16), pltpu.SemaphoreType.DMA((3,)),
         pltpu.VMEM((4, ROWS, CH), jnp.float32), pltpu.SemaphoreType.DMA((4,))], 3, "finish_zero", {3: 0},
    )


def narrow_body(x, out):
    for r in range(0, TAPS, TILE):
        out[r : r + TILE, :] = x[r : r + TILE, :].astype(jnp.bfloat16)


def narrow(x):
    return kernel_call(
        narrow_body, jax.ShapeDtypeStruct((TAPS, CH), jnp.bfloat16), VMEM, (x,), [VMEM], [], 0, "narrow"
    )


def send(value, pairs, axis="layer"):
    return lax.ppermute(value, axis, pairs)


def after(value, *before):
    return lax.optimization_barrier((value, *before))[0]


A0 = [4 * k for k in range(8)]


def per_device(first_state, guess_points, weights):
    first = first_state.reshape(ROWS, CH)
    guess = guess_points.reshape(ROWS, CH)
    w = weights.reshape(4, TAPS, CH)
    shift = [(i, i + 1) for i in range(31)]

    came = send(guess, shift)
    wide = w[0].astype(jnp.float32)
    w_chip = send(wide, [p for k in A0 for p in ((k, k + 1), (k + 2, k + 3))])
    w_z2 = send(wide, [(k + 2, k + 1) for k in A0])
    w_z3 = send(wide, [(k + 3, k + 1) for k in A0])
    w_even3 = send(wide, [(8 * x, 8 * x + 7) for x in range(1, 4)])

    relaxed = sweep(first, came, w)
    came = send(relaxed, shift)
    fine, out0, squares = resweep(first, came, w, relaxed)

    in0 = send(out0, [p for k in A0 for p in ((k, k + 1), (k + 2, k + 3))])
    q1 = one_coarse(in0, w, fine)
    came = send(q1, [(k + 1, k + 3) for k in A0])
    wn_chip = narrow(w_chip)
    fine_a0 = send(fine, [(k, k + 1) for k in A0])
    fine_a2 = send(fine, [(k + 2, k + 1) for k in A0])
    fine_a3 = send(fine, [(k + 3, k + 1) for k in A0])
    ends = two_coarse(came, wn_chip, w, in0, fine)
    ends_in = send(ends, [(k + 3, k + 5) for k in A0[:-1]])
    late = after(wide, ends)
    w_b0 = send(late, [(k, k + 3) for k in A0])
    wn_z2, wn_z3, wn_even3 = narrow(w_z2), narrow(w_z3), narrow(w_even3)
    made = group(first, ends_in, wn_chip, w, wn_z2, wn_z3, fine_a0, fine, fine_a2, fine_a3)

    in_a = send(made, [(5, 13), (9, 15), (17, 23), (25, 31)])
    in_b = send(made, [(5, 15), (9, 13), (17, 21), (25, 29)])
    got = send(made, [(k + 1, k + 3) for k in A0])
    w_even2 = send(after(w_even3, made), [(8 * x + 7, 8 * x + 5) for x in range(1, 4)])
    wn_b0 = narrow(w_b0)
    wn_even2 = narrow(w_even2)
    rest = after(wide, made, got)
    fine_late = after(fine, made, got)
    w_b1 = send(rest, [(k + 1, k + 3) for k in A0])
    fine_b0 = send(fine_late, [(k, k + 3) for k in A0])
    fine_b1 = send(fine_late, [(k + 1, k + 3) for k in A0])

    part = jnp.sum(after(squares, in_a, in_b)).reshape(1)
    part = part + send(part, [(0, 1), (1, 0), (2, 3), (3, 2)], "batch")
    part = part + send(part, [(0, 2), (2, 0), (1, 3), (3, 1)], "batch")
    norms = jnp.sqrt(part / (4 * ROWS * CH) + 1e-06)

    common = (in_b, in_a, wn_even2, wn_even3, wn_chip, wn_b0, made, got)
    ca1, cb1 = relay(in_a, in_b, *common)
    came = send(cb1, [(13, 21), (15, 23)])
    ca2, cb2 = relay(came, came, *common)
    came = send(cb2, [(21, 29), (23, 31)])
    carry = choose(ends, made, got, cb1, cb2)
    even_in = send(carry, [(3, 7), (5, 11), (7, 9), (13, 19), (15, 17), (21, 27), (23, 25)])
    wn_b1 = narrow(w_b1)
    out1, move, coarse = correct(
        first, ends_in, even_in, ca1, ca2, came, in_b, in_a, wn_even2, wn_even3, wn_chip, wn_b0, w, wn_b1,
        fine_a0, fine_b0, fine, fine_b1, made, got, ends,
    )
    in1 = send(out1, [p for k in A0 for p in ((k + 1, k), (k + 3, k + 2))])
    states = finish_one(move, coarse, w, wn_chip, in0, fine)
    states = finish_zero(in1, w, fine, states)
    return states.reshape(4, 1, SIDE, SIDE, CH), norms


def solution(mesh):
    placed = (
        P("batch", None, None, None),
        P("layer", "batch", None, None, None),
        P("layer", None, None, None, None),
    )
    return jax.shard_map(
        per_device,
        mesh=mesh,
        in_specs=placed,
        out_specs=(P("layer", "batch", None, None, None), P("layer")),
        check_vma=False,
    )
```

```python
import jax
import jax.numpy as jnp
from jax import lax
from jax.experimental import pallas as pl
from jax.experimental.pallas import tpu as pltpu
from jax.sharding import PartitionSpec as P


CH = 256
SIDE = 32
ROWS = SIDE * SIDE
TAPS = 9 * CH
TILE = 256
H = 2.0 / 128
STATE = jax.ShapeDtypeStruct((ROWS, CH), jnp.float32)
ANY = pl.BlockSpec(memory_space=pl.ANY)
HBM = pl.BlockSpec(memory_space=pltpu.HBM)
VMEM = pl.BlockSpec(memory_space=pltpu.VMEM)


def stencil_put(buf, r, value):
    rows = value.shape[0]
    column = lax.broadcasted_iota(jnp.int32, (rows, CH), 0) % SIDE
    before = jnp.where(column == 0, 0.0, pltpu.roll(value, 1, 0))
    behind = jnp.where(column == SIDE - 1, 0.0, pltpu.roll(value, rows - 1, 0))
    at = pl.ds(SIDE + r, rows)
    buf[at, 0:CH] = before.astype(jnp.bfloat16)
    buf[at, CH : 2 * CH] = value.astype(jnp.bfloat16)
    buf[at, 2 * CH : 3 * CH] = behind.astype(jnp.bfloat16)


def stencil_pads(*bufs):
    zero = jnp.zeros((SIDE, 3 * CH), jnp.bfloat16)
    for buf in bufs:
        buf[0:SIDE, :] = zero
        buf[SIDE + ROWS :, :] = zero


def relu_conv(buf, weight, r):
    total = None
    for dy in range(3):
        part = jnp.dot(
            buf[pl.ds(r + SIDE * dy, TILE), :],
            weight[pl.ds(3 * CH * dy, 3 * CH), :],
            preferred_element_type=jnp.float32,
        )
        total = part if total is None else total + part
    return jnp.maximum(total, 0.0)


def run_steps(start, bufs, held, steps):
    for r in range(0, ROWS, TILE):
        stencil_put(bufs[0], r, start(r))
    for n, (ready, weight, update) in enumerate(steps):
        ready()
        source, target = bufs[n % 2], bufs[(n + 1) % 2]
        for r in range(0, ROWS, TILE):
            current = start(r) if n == 0 else held[r : r + TILE, :]
            value = update(r, current, relu_conv(source, weight, r))
            if n + 1 < len(steps):
                held[r : r + TILE, :] = value
                stencil_put(target, r, value)


SCRATCH = (
    pltpu.VMEM((ROWS + 2 * SIDE, 3 * CH), jnp.bfloat16),
    pltpu.VMEM((ROWS + 2 * SIDE, 3 * CH), jnp.bfloat16),
    pltpu.VMEM((ROWS, CH), jnp.float32),
)


class Load:
    def __init__(self, choices, target, sem):
        self.choices, self.target, self.sem = choices, target, sem

    def start(self):
        for condition, source in self.choices:
            if condition is None:
                pltpu.make_async_copy(source, self.target, self.sem).start()
                continue

            @pl.when(condition)
            def _(source=source):
                pltpu.make_async_copy(source, self.target, self.sem).start()

    def wait(self):
        pltpu.make_async_copy(self.choices[0][1], self.target, self.sem).wait()


def plain(source, target, sem):
    return Load([(None, source)], target, sem)


def start_all(*loads):
    for load in loads:
        load.start()


def wait_all(*loads):
    for load in loads:
        load.wait()


def rows(ref):
    return lambda r: ref[r : r + TILE, :]


def either(condition, yes, no):
    return lambda r: jnp.where(condition, yes[r : r + TILE, :], no[r : r + TILE, :])


def ready(waits, starts=()):
    def run():
        wait_all(*waits)
        start_all(*starts)

    return run


def spot():
    d = lax.axis_index("layer")
    return d, d // 8, (d // 2) % 4, d % 2


def nothing():
    return None


def kernel_call(body, outs, out_specs, args, in_specs, scratch, convs, grant, aliases=None):
    return pl.pallas_call(
        body,
        out_shape=outs,
        in_specs=in_specs,
        out_specs=out_specs,
        scratch_shapes=scratch,
        input_output_aliases=aliases or {},
        compiler_params=pltpu.CompilerParams(vmem_limit_bytes=grant << 20),
        cost_estimate=pl.CostEstimate(flops=convs * 2 * ROWS * TAPS * CH, bytes_accessed=4 << 20, transcendentals=0),
    )(*args)


def room(n):
    return [pltpu.VMEM((n, ROWS, CH), jnp.float32), pltpu.SemaphoreType.DMA((n,))]


def wbuf(n):
    return [pltpu.VMEM((n, TAPS, CH), jnp.bfloat16), pltpu.SemaphoreType.DMA((n,))]


def sweep_body(first, given, w, out, b0, b1, held, xv, xs, wv, ws):
    d = lax.axis_index("layer")
    x = xv.at[0]
    got = Load([(d == 0, first), (d != 0, given)], x, xs.at[0])
    ww = [plain(w.at[n], wv.at[n], ws.at[n]) for n in range(4)]
    start_all(got, ww[0])
    stencil_pads(b0, b1)
    got.wait()

    def layer(r, v, a):
        return v + H * a

    def last(r, v, a):
        out[r : r + TILE, :] = v + H * a

    run_steps(
        rows(x), (b0, b1), held,
        [(ready(ww[n : n + 1], ww[n + 1 : n + 2]), wv.at[n], layer if n < 3 else last) for n in range(4)],
    )


def sweep(first, given, w):
    return kernel_call(
        sweep_body, STATE, VMEM, (first, given, w), [ANY, ANY, HBM], [*SCRATCH, *room(1), *wbuf(4)], 4, 16
    )


def resweep_body(first, given, w, relaxed, fine, send, squares, b0, b1, held, ahead, xv, xs, wv, ws):
    d = lax.axis_index("layer")
    x = xv.at[0]
    got = Load([(d == 0, first), (d != 0, given)], x, xs.at[0])
    ww = [plain(w.at[n], wv.at[n], ws.at[n]) for n in range(4)]
    start_all(got, ww[0])
    stencil_pads(b0, b1)
    squares[...] = jnp.zeros_like(squares)
    got.wait()

    def head(r, v, a):
        ahead[r : r + TILE, :] = v + 4 * H * a
        return v + H * a

    def layer(r, v, a):
        return v + H * a

    def last(r, v, a):
        value = v + H * a
        rhs = value - ahead[r : r + TILE, :]
        fine[r : r + TILE, :] = rhs
        off = value - relaxed[r : r + TILE, :]
        squares[...] += jnp.sum((off * off).reshape(TILE // 8, 8, CH), axis=0)
        send[r : r + TILE, :] = jnp.where(d % 4 < 2, value, rhs)

    run_steps(
        rows(x), (b0, b1), held,
        [(ready(ww[n : n + 1], ww[n + 1 : n + 2]), wv.at[n], (head, layer, layer, last)[n]) for n in range(4)],
    )


def resweep(first, given, w, relaxed):
    return kernel_call(
        resweep_body, (STATE, STATE, jax.ShapeDtypeStruct((8, CH), jnp.float32)), (VMEM,) * 3,
        (first, given, w, relaxed), [ANY, ANY, HBM, VMEM],
        [*SCRATCH, pltpu.VMEM((ROWS, CH), jnp.float32), *room(1), *wbuf(4)], 4, 20,
    )


def coarse_update(rhs):
    return lambda r, v, a: v + 4 * H * a + rhs[r : r + TILE, :]


def coarse_last(rhs, out):
    def update(r, v, a):
        out[r : r + TILE, :] = v + 4 * H * a + rhs[r : r + TILE, :]

    return update


def one_coarse_body(x, w, rhs, out, b0, b1, held, fv, fs, wv, ws):
    ww = plain(w.at[0], wv.at[0], ws.at[0])
    ff = plain(rhs, fv.at[0], fs.at[0])
    start_all(ww, ff)
    stencil_pads(b0, b1)
    run_steps(rows(x), (b0, b1), held, [(ready([ww, ff]), wv.at[0], coarse_last(fv.at[0], out))])


def one_coarse(x, w, rhs):
    return kernel_call(
        one_coarse_body, STATE, VMEM, (x, w, rhs), [VMEM, HBM, ANY], [*SCRATCH, *room(1), *wbuf(1)], 1,
        14,
    )


def two_coarse_body(x, wa, w, rhs_a, rhs_b, out, b0, b1, held, fv, fs, wv, ws):
    ww = [plain(wa, wv.at[0], ws.at[0]), plain(w.at[0], wv.at[1], ws.at[1])]
    ff = [plain(rhs_a, fv.at[0], fs.at[0]), plain(rhs_b, fv.at[1], fs.at[1])]
    start_all(ww[0], ff[0])
    stencil_pads(b0, b1)
    run_steps(
        rows(x), (b0, b1), held,
        [(ready([ww[0], ff[0]], [ww[1], ff[1]]), wv.at[0], coarse_update(fv.at[0])),
         (ready([ww[1], ff[1]]), wv.at[1], coarse_last(fv.at[1], out))],
    )


def two_coarse(x, wa, w, rhs_a, rhs_b):
    return kernel_call(
        two_coarse_body, STATE, VMEM, (x, wa, w, rhs_a, rhs_b), [VMEM, ANY, HBM, ANY, ANY],
        [*SCRATCH, *room(2), *wbuf(2)], 2, 16,
    )


def group_body(first, ends, w0, w1, w2, w3, f0, f1, f2, f3, out, b0, b1, held, ahead, xv, xs, wv, ws):
    d = lax.axis_index("layer")
    x = xv.at[4]
    got = Load([(d == 1, first), (d != 1, ends)], x, xs.at[4])
    ww = [plain(s, wv.at[n], ws.at[n]) for n, s in enumerate((w0, w1.at[0], w2, w3))]
    ff = [plain(s, xv.at[n], xs.at[n]) for n, s in enumerate((f0, f1, f2, f3))]
    start_all(got, ww[0], ff[0])
    stencil_pads(b0, b1)
    got.wait()

    def head(r, v, a):
        ahead[r : r + TILE, :] = v + 16 * H * a
        return v + 4 * H * a + xv[0, r : r + TILE, :]

    def last(r, v, a):
        value = v + 4 * H * a + xv[3, r : r + TILE, :]
        out[r : r + TILE, :] = jnp.where(d == 5, value, value - ahead[r : r + TILE, :])

    updates = (head, coarse_update(xv.at[1]), coarse_update(xv.at[2]), last)
    run_steps(
        rows(x), (b0, b1), held,
        [(ready([ww[n], ff[n]], ww[n + 1 : n + 2] + ff[n + 1 : n + 2]), wv.at[n], updates[n]) for n in range(4)],
    )


def group(*args):
    return kernel_call(
        group_body, STATE, VMEM, args, [ANY] * 3 + [HBM] + [ANY] * 6,
        [*SCRATCH, pltpu.VMEM((ROWS, CH), jnp.float32), *room(5), *wbuf(4)], 4, 22,
    )


def relay_body(came2, came3, rhs2, rhs3, we2, we3, w02, w03, own2, own3, ca, cb, b0, b1, held, wv, ws):
    _, _, z, _ = spot()
    third = z == 3
    other = z != 3
    x, ra, rb = either(third, came3, came2), either(third, rhs3, rhs2), either(third, own3, own2)
    got_wa = Load([(third, we3), (other, we2)], wv.at[0], ws.at[0])
    got_wb = Load([(third, w03), (other, w02)], wv.at[1], ws.at[1])
    start_all(got_wa, got_wb)
    stencil_pads(b0, b1)

    def first(r, v, a):
        value = v + 16 * H * a + ra(r)
        ca[r : r + TILE, :] = value
        return value

    def second(r, v, a):
        cb[r : r + TILE, :] = v + 16 * H * a + rb(r)

    run_steps(
        x, (b0, b1), held, [(ready([got_wa]), wv.at[0], first), (ready([got_wb]), wv.at[1], second)]
    )


def relay(*args):
    return kernel_call(
        relay_body, (STATE, STATE), (VMEM, VMEM), args, [VMEM] * 4 + [ANY] * 4 + [VMEM] * 2, [*SCRATCH, *wbuf(2)], 2,
        16,
    )


def choose_body(ends, made, got, cb1, cb2, out, sem):
    _, x, z, _ = spot()
    load = Load([((x == 0) & (z < 2), ends), ((x == 0) & (z == 2), made), ((x == 0) & (z == 3), got),
                 (x == 1, cb1), (x >= 2, cb2)], out, sem)
    load.start()
    load.wait()


def choose(*args):
    return kernel_call(choose_body, STATE, VMEM, args, [ANY] * 5, [pltpu.SemaphoreType.DMA], 0, 8)


def correct_body(first, ends_in, even_in, ca1, ca2, came, rhs2, rhs3, we2, we3, wa0, wb0, wa1, wb1,
                 fa0, fb0, fa1, fb1, made, got, ends, send, move, coarse, b0, b1, held, xv, xs, wv, ws):
    d, xc, z, _ = spot()
    is_a = z % 2 == 0
    is_b = z % 2 == 1
    odd = z >= 2
    third = z == 3
    other = z != 3
    late = (xc == 3) & odd
    x, ra, g0, g1, rk = (xv.at[n] for n in range(5))
    got_x = Load(
        [((xc == 0) & (z < 2), first), ((xc == 0) & (z == 2), ends_in),
         (((xc == 0) & third) | ((xc > 0) & (z < 2)), even_in),
         ((xc == 1) & odd, ca1), ((xc == 2) & odd, ca2), (late, came)], x, xs.at[0])
    got_e = Load([(third, we3), (other, we2)], wv.at[0], ws.at[0])
    got_ra = Load([(third, rhs3), (other, rhs2)], ra, xs.at[1])
    got_w0 = Load([(is_a, wa0), (is_b, wb0)], wv.at[1], ws.at[1])
    got_w1 = Load([(is_a, wa1.at[0]), (is_b, wb1)], wv.at[2], ws.at[2])
    got_f0 = Load([(is_a, fa0), (is_b, fb0)], g0, xs.at[2])
    got_f1 = Load([(is_a, fa1), (is_b, fb1)], g1, xs.at[3])
    got_r = Load([(is_a, made), (is_b & (d // 4 > 0), got), (is_b & (d // 4 == 0), ends)], rk, xs.at[4])
    start_all(got_x, got_e, got_ra)
    stencil_pads(b0, b1)
    got_x.wait()
    wait_all(got_e, got_ra)
    start_all(got_w0, got_f0, got_r, got_w1, got_f1)

    @pl.when(late)
    def _():
        def update(r, v, a):
            held[r : r + TILE, :] = v + 16 * H * a + ra[r : r + TILE, :]

        run_steps(rows(x), (b0, b1), held, [(nothing, wv.at[0], update)])
        x[...] = held[...]

    def zero(r, v, a):
        rk_rows = rk[r : r + TILE, :]
        coarse[r : r + TILE, :] = jnp.where(d // 4 < 2, rk_rows, v + 16 * H * a + rk_rows)
        value = v + 4 * H * a + g0[r : r + TILE, :]
        move[r : r + TILE, :] = value
        send[r : r + TILE, :] = v
        return value

    def one(r, v, a):
        @pl.when(is_b)
        def _():
            value = v + 4 * H * a + g1[r : r + TILE, :]
            move[r : r + TILE, :] = value
            send[r : r + TILE, :] = value

    run_steps(
        rows(x), (b0, b1), held,
        [(ready([got_w0, got_f0, got_r]), wv.at[1], zero), (ready([got_w1, got_f1]), wv.at[2], one)],
    )


def correct(*args):
    return kernel_call(
        correct_body, (STATE,) * 3, (VMEM,) * 3, args, [ANY] * 12 + [HBM] + [ANY] * 8,
        [*SCRATCH, *room(5), *wbuf(3)], 3, 22
    )


def finish(x, rhs, out, stage, os, bufs, held, wv, ww, last_state):
    copies = [pltpu.make_async_copy(stage.at[n], out.at[n], os.at[n]) for n in range(4)]

    def layer(n):
        def update(r, v, a):
            value = v + H * a
            stage[n, r : r + TILE, :] = value
            if n == 0:
                coarse = v + 4 * H * a + rhs[r : r + TILE, :]
                stage[3, r : r + TILE, :] = coarse if last_state is None else last_state(r, coarse)
            if r + TILE == ROWS:
                copies[n].start()
                if n == 0:
                    copies[3].start()
            return value

        return update

    run_steps(
        rows(x), bufs, held, [(ready(ww[n : n + 1], ww[n + 1 : n + 2]), wv.at[n], layer(n)) for n in range(3)]
    )
    for copy in copies:
        copy.wait()


def finish_one_body(x, coarse, w, w2, f2, rhs, out, b0, b1, held, fv, fs, wv, ws, w2v, stage, os):
    _, _, z, core = spot()
    is_b = z % 2 == 1

    @pl.when(core == 1)
    def _():
        ww = [plain(w.at[n], wv.at[n], ws.at[n]) for n in range(3)]
        got_w2 = plain(w2, w2v, ws.at[3])
        got_f2 = plain(f2, fv.at[1], fs.at[1])
        got_rhs = plain(rhs, fv.at[2], fs.at[2])
        start_all(got_w2, got_f2)
        stencil_pads(b0, b1)
        wait_all(got_w2, got_f2)
        start_all(ww[0], got_rhs)
        xb = fv.at[0]

        @pl.when(is_b)
        def _():
            def update(r, v, a):
                xb[r : r + TILE, :] = v + 4 * H * a + fv[1, r : r + TILE, :]

            run_steps(rows(x), (b0, b1), held, [(nothing, w2v, update)])

        @pl.when(jnp.logical_not(is_b))
        def _():
            xb[...] = x[...]

        def last_state(r, value):
            return jnp.where(is_b, coarse[r : r + TILE, :], value)

        got_rhs.wait()
        finish(xb, fv.at[2], out, stage, os, (b0, b1), held, wv, ww, last_state)


OUT = jax.ShapeDtypeStruct((4, ROWS, CH), jnp.float32)


def finish_one(x, coarse, w, w2, f2, rhs):
    return kernel_call(
        finish_one_body, OUT, ANY, (x, coarse, w, w2, f2, rhs), [VMEM, VMEM, HBM, ANY, ANY, ANY],
        [*SCRATCH, *room(3), pltpu.VMEM((3, TAPS, CH), jnp.bfloat16),
         pltpu.SemaphoreType.DMA((4,)), pltpu.VMEM((TAPS, CH), jnp.bfloat16),
         pltpu.VMEM((4, ROWS, CH), jnp.float32), pltpu.SemaphoreType.DMA((4,))], 4, 22,
    )


def finish_zero_body(x, w, rhs, so_far, out, b0, b1, held, fv, fs, wv, ws, stage, os):
    _, _, _, core = spot()

    @pl.when(core == 0)
    def _():
        ww = [plain(w.at[n], wv.at[n], ws.at[n]) for n in range(3)]
        got = plain(x, fv.at[0], fs.at[0])
        got_rhs = plain(rhs, fv.at[1], fs.at[1])
        start_all(got, ww[0], got_rhs)
        stencil_pads(b0, b1)
        wait_all(got, got_rhs)
        finish(fv.at[0], fv.at[1], out, stage, os, (b0, b1), held, wv, ww, None)


def finish_zero(x, w, rhs, so_far):
    return kernel_call(
        finish_zero_body, OUT, ANY, (x, w, rhs, so_far), [ANY, HBM, ANY, ANY],
        [*SCRATCH, *room(2), *wbuf(3), pltpu.VMEM((4, ROWS, CH), jnp.float32), pltpu.SemaphoreType.DMA((4,))], 3,
        20, {3: 0},
    )


def widen_body(w, out, wv, sem):
    load = plain(w.at[0], wv, sem)
    load.start()
    load.wait()
    for r in range(0, TAPS, TILE):
        out[r : r + TILE, :] = wv[r : r + TILE, :].astype(jnp.float32)


def widen(w):
    return kernel_call(
        widen_body, jax.ShapeDtypeStruct((TAPS, CH), jnp.float32), VMEM, (w,), [HBM],
        [pltpu.VMEM((TAPS, CH), jnp.bfloat16), pltpu.SemaphoreType.DMA], 0, 8,
    )


def norm_sum_body(a, b, out):
    out[...] = a[...] + b[...]


def norm_sum(a, b):
    return kernel_call(norm_sum_body, jax.ShapeDtypeStruct((8, CH), jnp.float32), VMEM, (a, b), [VMEM, VMEM], [], 0, 2)


def norm_root_body(a, b, out):
    total = jnp.sum(a[...] + b[...])
    root = jnp.sqrt(jnp.full((8, 128), total, jnp.float32) / (4 * ROWS * CH) + 1e-06)
    out[0] = jnp.max(root)


def norm_root(a, b):
    return kernel_call(
        norm_root_body, jax.ShapeDtypeStruct((1,), jnp.float32), pl.BlockSpec(memory_space=pltpu.SMEM), (a, b),
        [VMEM, VMEM], [], 0, 2,
    )


def narrow_body(x, out):
    for r in range(0, TAPS, TILE):
        out[r : r + TILE, :] = x[r : r + TILE, :].astype(jnp.bfloat16)


def narrow(x):
    return kernel_call(narrow_body, jax.ShapeDtypeStruct((TAPS, CH), jnp.bfloat16), VMEM, (x,), [VMEM], [], 0, 8)


PART = TAPS // 4


def pack_body(chip, own, narrowed, out):
    at = pl.ds(pl.multiple_of(lax.axis_index("batch") * PART, 64), PART)
    out[0:PART, :] = chip[at, :]
    out[PART:, :] = own[at, :]
    for r in range(0, TAPS, TILE):
        narrowed[r : r + TILE, :] = chip[r : r + TILE, :].astype(jnp.bfloat16)


def pack(chip, own):
    return kernel_call(
        pack_body, (jax.ShapeDtypeStruct((TAPS, CH), jnp.bfloat16), jax.ShapeDtypeStruct((2 * PART, CH), jnp.float32)),
        (VMEM, VMEM), (chip, own), [VMEM, VMEM], [], 0, 8,
    )


def unpack_body(p0, p1, p2, p3, out0, out1):
    y = lax.axis_index("batch")
    for n, part in enumerate((p0, p1, p2, p3)):
        at = pl.ds(pl.multiple_of((y + 4 - n) % 4 * PART, 64), PART)
        out0[at, :] = part[0:PART, :].astype(jnp.bfloat16)
        out1[at, :] = part[PART:, :].astype(jnp.bfloat16)


def unpack(*parts):
    kernel = jax.ShapeDtypeStruct((TAPS, CH), jnp.bfloat16)
    return kernel_call(unpack_body, (kernel, kernel), (VMEM, VMEM), parts, [VMEM] * 4, [], 0, 10)


def send(value, pairs, axis="layer"):
    return lax.ppermute(value, axis, pairs)


A0 = [4 * k for k in range(8)]


def cycle(first_state, guess_points, weights):
    first = first_state.reshape(ROWS, CH)
    guess = guess_points.reshape(ROWS, CH)
    w = weights.reshape(4, TAPS, CH)
    shift = [(i, i + 1) for i in range(31)]

    came = send(guess, shift)
    wide = widen(w)
    w_chip = send(wide, [p for k in A0 for p in ((k, k + 1), (k + 2, k + 3))])
    w_z2 = send(wide, [(k + 2, k + 1) for k in A0])
    wn_chip, packed = pack(w_chip, wide)
    part0 = send(packed, [(k + 1, k + 3) for k in A0])
    relaxed = sweep(first, came, w)

    came = send(relaxed, shift)
    w_z3 = send(wide, [(k + 3, k + 1) for k in A0])
    w_even3 = send(wide, [(8 * x, 8 * x + 7) for x in range(1, 4)])
    fine, out0, squares = resweep(first, came, w, relaxed)

    in0 = send(out0, [p for k in A0 for p in ((k, k + 1), (k + 2, k + 3))])
    q1 = one_coarse(in0, w, fine)
    came = send(q1, [(k + 1, k + 3) for k in A0])
    fine_a2 = send(fine, [(k + 2, k + 1) for k in A0])
    fine_a3 = send(fine, [(k + 3, k + 1) for k in A0])
    fine_a0 = send(fine, [(k, k + 1) for k in A0])
    parts = [part0]
    for n in range(1, 4):
        ring = [((k + 3) * 4 + y, (k + 3) * 4 + (y + n) % 4) for k in A0 for y in range(4)]
        parts.append(send(part0, ring, ("layer", "batch")))
    ends = two_coarse(came, wn_chip, w, in0, fine)

    ends_in = send(ends, [(k + 3, k + 5) for k in A0[:-1]])
    fine_b0 = send(fine, [(k, k + 3) for k in A0])
    fine_b1 = send(fine, [(k + 1, k + 3) for k in A0])
    wn_z2, wn_z3, wn_even3 = narrow(w_z2), narrow(w_z3), narrow(w_even3)
    w_even2 = send(w_even3, [(8 * x + 7, 8 * x + 5) for x in range(1, 4)])
    made = group(first, ends_in, wn_chip, w, wn_z2, wn_z3, fine_a0, fine, fine_a2, fine_a3)

    in_a = send(made, [(5, 13), (9, 15), (17, 23), (25, 31)])
    in_b = send(made, [(5, 15), (9, 13), (17, 21), (25, 29)])
    got = send(made, [(k + 1, k + 3) for k in A0])
    wn_b0, wn_b1 = unpack(*parts)
    wn_even2 = narrow(w_even2)

    common = (in_b, in_a, wn_even2, wn_even3, wn_chip, wn_b0, made, got)
    ca1, cb1 = relay(in_a, in_b, *common)
    came = send(cb1, [(13, 21), (15, 23)])
    swapped = send(squares, [(0, 1), (1, 0), (2, 3), (3, 2)], "batch")
    squares = norm_sum(squares, swapped)
    swapped = send(squares, [(0, 2), (2, 0), (1, 3), (3, 1)], "batch")
    norms = norm_root(squares, swapped)
    ca2, cb2 = relay(came, came, *common)
    came = send(cb2, [(21, 29), (23, 31)])
    carry = choose(ends, made, got, cb1, cb2)
    even_in = send(carry, [(3, 7), (5, 11), (7, 9), (13, 19), (15, 17), (21, 27), (23, 25)])
    out1, move, coarse = correct(
        first, ends_in, even_in, ca1, ca2, came, in_b, in_a, wn_even2, wn_even3, wn_chip, wn_b0, w, wn_b1,
        fine_a0, fine_b0, fine, fine_b1, made, got, ends,
    )
    in1 = send(out1, [p for k in A0 for p in ((k + 1, k), (k + 3, k + 2))])
    states = finish_one(move, coarse, w, wn_chip, in0, fine)
    states = finish_zero(in1, w, fine, states)
    return states.reshape(4, 1, SIDE, SIDE, CH), norms


def solution(mesh):
    placed = (
        P("batch", None, None, None),
        P("layer", "batch", None, None, None),
        P("layer", None, None, None, None),
    )
    return jax.shard_map(
        cycle,
        mesh=mesh,
        in_specs=placed,
        out_specs=(P("layer", "batch", None, None, None), P("layer")),
        check_vma=False,
    )
```

```python
import jax
import jax.numpy as jnp
from jax import lax
from jax.experimental import pallas as pl
from jax.experimental.pallas import tpu as pltpu
from jax.sharding import PartitionSpec as P


CH = 256
SIDE = 32
ROWS = SIDE * SIDE
TAPS = 9 * CH
TILE = 256
H = 2.0 / 128
STATE = jax.ShapeDtypeStruct((ROWS, CH), jnp.float32)
ANY = pl.BlockSpec(memory_space=pl.ANY)
HBM = pl.BlockSpec(memory_space=pltpu.HBM)
VMEM = pl.BlockSpec(memory_space=pltpu.VMEM)


def stencil_put(buf, r, value):
    rows = value.shape[0]
    cube = value.reshape(rows // SIDE, SIDE, CH)
    column = lax.broadcasted_iota(jnp.int32, (1, SIDE, CH), 1)
    before = jnp.where(column == 0, 0.0, pltpu.roll(cube, 1, 1)).reshape(rows, CH)
    behind = jnp.where(column == SIDE - 1, 0.0, pltpu.roll(cube, SIDE - 1, 1)).reshape(rows, CH)
    at = pl.ds(SIDE + r, rows)
    buf[at, 0:CH] = before.astype(jnp.bfloat16)
    buf[at, CH : 2 * CH] = value.astype(jnp.bfloat16)
    buf[at, 2 * CH : 3 * CH] = behind.astype(jnp.bfloat16)


def stencil_pads(*bufs):
    zero = jnp.zeros((SIDE, 3 * CH), jnp.bfloat16)
    for buf in bufs:
        buf[0:SIDE, :] = zero
        buf[SIDE + ROWS :, :] = zero


def relu_conv(buf, weight, r):
    total = None
    for dy in range(3):
        part = jnp.dot(
            buf[pl.ds(r + SIDE * dy, TILE), :],
            weight[pl.ds(3 * CH * dy, 3 * CH), :],
            preferred_element_type=jnp.float32,
        )
        total = part if total is None else total + part
    return jnp.maximum(total, 0.0)


def run_steps(start, bufs, held, steps):
    @pl.loop(0, ROWS // TILE)
    def _(i):
        r = pl.multiple_of(i * TILE, TILE)
        stencil_put(bufs[0], r, start(r))

    for n, (ready, weight, update) in enumerate(steps):
        ready()
        source, target = bufs[n % 2], bufs[(n + 1) % 2]
        for r in range(0, ROWS, TILE):
            current = start(r) if n == 0 else held[r : r + TILE, :]
            value = update(r, current, relu_conv(source, weight, r))
            if n + 1 < len(steps):
                held[r : r + TILE, :] = value
                stencil_put(target, r, value)


def run_pairs(start, bufs, held, copies, weights, update):
    @pl.loop(0, ROWS // TILE)
    def _(i):
        r = pl.multiple_of(i * TILE, TILE)
        value = start(r)
        held[pl.ds(r, TILE), :] = value
        stencil_put(bufs[0], r, value)

    @pl.loop(0, 2)
    def _(turn):
        for slot in range(2):
            copies(2 * turn + slot).wait()
            for r in range(0, ROWS, TILE):
                a = relu_conv(bufs[slot], weights.at[2 * turn + slot], r)
                value = update(turn, slot, r, held[r : r + TILE, :], a)
                held[r : r + TILE, :] = value
                stencil_put(bufs[1 - slot], r, value)


SCRATCH = (
    pltpu.VMEM((ROWS + 2 * SIDE, 3 * CH), jnp.bfloat16),
    pltpu.VMEM((ROWS + 2 * SIDE, 3 * CH), jnp.bfloat16),
    pltpu.VMEM((ROWS, CH), jnp.float32),
)


class Load:
    def __init__(self, choices, target, sem):
        self.choices, self.target, self.sem = choices, target, sem

    def start(self):
        for condition, source in self.choices:
            if condition is None:
                pltpu.make_async_copy(source, self.target, self.sem).start()
                continue

            @pl.when(condition)
            def _(source=source):
                pltpu.make_async_copy(source, self.target, self.sem).start()

    def wait(self):
        pltpu.make_async_copy(self.choices[0][1], self.target, self.sem).wait()


def plain(source, target, sem):
    return Load([(None, source)], target, sem)


def start_all(*loads):
    for load in loads:
        load.start()


def wait_all(*loads):
    for load in loads:
        load.wait()


def rows(ref):
    return lambda r: ref[pl.ds(r, TILE), :]


def either(condition, yes, no):
    return lambda r: jnp.where(condition, yes[pl.ds(r, TILE), :], no[pl.ds(r, TILE), :])


def ready(waits, starts=()):
    def run():
        wait_all(*waits)
        start_all(*starts)

    return run


def spot():
    d = lax.axis_index("layer")
    return d, d // 8, (d // 2) % 4, d % 2


def nothing():
    return None


def kernel_call(body, outs, out_specs, args, in_specs, scratch, convs, grant, aliases=None):
    return pl.pallas_call(
        body,
        out_shape=outs,
        in_specs=in_specs,
        out_specs=out_specs,
        scratch_shapes=scratch,
        input_output_aliases=aliases or {},
        compiler_params=pltpu.CompilerParams(vmem_limit_bytes=grant << 20),
        cost_estimate=pl.CostEstimate(flops=convs * 2 * ROWS * TAPS * CH, bytes_accessed=4 << 20, transcendentals=0),
    )(*args)


def room(n):
    return [pltpu.VMEM((n, ROWS, CH), jnp.float32), pltpu.SemaphoreType.DMA((n,))]


def wbuf(n):
    return [pltpu.VMEM((n, TAPS, CH), jnp.bfloat16), pltpu.SemaphoreType.DMA((n,))]


def sweep_body(first, given, w, out, b0, b1, wv, ws):
    x = either(lax.axis_index("layer") == 0, first, given)

    def copies(n):
        return pltpu.make_async_copy(w.at[n], wv.at[n], ws.at[n])

    start_all(*(copies(n) for n in range(4)))
    stencil_pads(b0, b1)
    run_pairs(x, (b0, b1), out, copies, wv, lambda turn, slot, r, v, a: v + H * a)


def sweep(first, given, w):
    return kernel_call(sweep_body, STATE, VMEM, (first, given, w), [VMEM, VMEM, HBM], [*SCRATCH[:2], *wbuf(4)], 4, 16)


def resweep_body(first, given, w, relaxed, fine, send, squares, b0, b1, held, ahead, sums, wv, ws):
    d = lax.axis_index("layer")
    x = either(d == 0, first, given)

    def copies(n):
        return pltpu.make_async_copy(w.at[n], wv.at[n], ws.at[n])

    start_all(*(copies(n) for n in range(4)))
    stencil_pads(b0, b1)
    sums[...] = jnp.zeros_like(sums)

    def update(turn, slot, r, v, a):
        value = v + H * a
        at = slice(r, r + TILE)
        if slot == 0:
            ahead[turn, at, :] = v + 4 * H * a
            return value
        rhs = value - ahead[0, at, :]
        fine[at, :] = rhs
        off = value - relaxed[at, :]
        sums[turn] += jnp.sum((off * off).reshape(TILE // 8, 8, CH), axis=0)
        send[at, :] = jnp.where(d % 4 < 2, value, rhs)
        return value

    run_pairs(x, (b0, b1), held, copies, wv, update)
    squares[...] = sums[1]


def resweep(first, given, w, relaxed):
    return kernel_call(
        resweep_body, (STATE, STATE, jax.ShapeDtypeStruct((8, CH), jnp.float32)), (VMEM,) * 3,
        (first, given, w, relaxed), [VMEM, VMEM, HBM, VMEM],
        [*SCRATCH, pltpu.VMEM((2, ROWS, CH), jnp.float32), pltpu.VMEM((2, 8, CH), jnp.float32), *wbuf(4)], 4,
        20,
    )


def coarse_update(rhs):
    return lambda r, v, a: v + 4 * H * a + rhs[r : r + TILE, :]


def coarse_last(rhs, out):
    def update(r, v, a):
        out[r : r + TILE, :] = v + 4 * H * a + rhs[r : r + TILE, :]

    return update


def one_coarse_body(x, w, rhs, out, b0, b1, held, fv, fs, wv, ws):
    ww = plain(w.at[0], wv.at[0], ws.at[0])
    ff = plain(rhs, fv.at[0], fs.at[0])
    start_all(ww, ff)
    stencil_pads(b0, b1)
    run_steps(rows(x), (b0, b1), held, [(ready([ww, ff]), wv.at[0], coarse_last(fv.at[0], out))])


def one_coarse(x, w, rhs):
    return kernel_call(
        one_coarse_body, STATE, VMEM, (x, w, rhs), [VMEM, HBM, ANY], [*SCRATCH, *room(1), *wbuf(1)], 1,
        14,
    )


def two_coarse_body(x, wa, w, rhs_a, rhs_b, out, b0, b1, held, fv, fs, wv, ws):
    ww = [plain(wa, wv.at[0], ws.at[0]), plain(w.at[0], wv.at[1], ws.at[1])]
    ff = [plain(rhs_a, fv.at[0], fs.at[0]), plain(rhs_b, fv.at[1], fs.at[1])]
    start_all(ww[0], ff[0])
    stencil_pads(b0, b1)
    run_steps(
        rows(x), (b0, b1), held,
        [(ready([ww[0], ff[0]], [ww[1], ff[1]]), wv.at[0], coarse_update(fv.at[0])),
         (ready([ww[1], ff[1]]), wv.at[1], coarse_last(fv.at[1], out))],
    )


def two_coarse(x, wa, w, rhs_a, rhs_b):
    return kernel_call(
        two_coarse_body, STATE, VMEM, (x, wa, w, rhs_a, rhs_b), [VMEM, ANY, HBM, ANY, ANY],
        [*SCRATCH, *room(2), *wbuf(2)], 2, 16,
    )


def group_body(first, ends, w0, w1, w2, w3, f0, f1, f2, f3, out, b0, b1, held, ahead, fv, fs, wv, ws):
    d = lax.axis_index("layer")
    x = either(d == 1, first, ends)
    ww = [plain(s, wv.at[n], ws.at[n]) for n, s in enumerate((w0, w1.at[0], w2, w3))]
    ff = [plain(s, fv.at[n], fs.at[n]) for n, s in enumerate((f0, f1, f2, f3))]
    for n in range(4):
        start_all(ww[n], ff[n])
    stencil_pads(b0, b1)

    class copies:
        def __init__(self, n):
            self.n = n

        def wait(self):
            pltpu.make_async_copy(w0, wv.at[self.n], ws.at[self.n]).wait()
            pltpu.make_async_copy(f0, fv.at[self.n], fs.at[self.n]).wait()

    def update(turn, slot, r, v, a):
        at = slice(r, r + TILE)
        value = v + 4 * H * a + fv[2 * turn + slot, at, :]
        if slot == 0:
            ahead[turn, at, :] = v + 16 * H * a
        else:
            out[at, :] = jnp.where(d == 5, value, value - ahead[0, at, :])
        return value

    run_pairs(x, (b0, b1), held, copies, wv, update)


def group(*args):
    return kernel_call(
        group_body, STATE, VMEM, args, [VMEM, VMEM, ANY, HBM] + [ANY] * 6,
        [*SCRATCH, pltpu.VMEM((2, ROWS, CH), jnp.float32), *room(4), *wbuf(4)], 4, 22,
    )


def relay_body(came2, came3, rhs2, rhs3, we2, we3, w02, w03, own2, own3, ca, cb, b0, b1, held, wv, ws):
    _, _, z, _ = spot()
    third = z == 3
    other = z != 3
    x, ra, rb = either(third, came3, came2), either(third, rhs3, rhs2), either(third, own3, own2)
    got_wa = Load([(third, we3), (other, we2)], wv.at[0], ws.at[0])
    got_wb = Load([(third, w03), (other, w02)], wv.at[1], ws.at[1])
    start_all(got_wa, got_wb)
    stencil_pads(b0, b1)

    def first(r, v, a):
        value = v + 16 * H * a + ra(r)
        ca[r : r + TILE, :] = value
        return value

    def second(r, v, a):
        cb[r : r + TILE, :] = v + 16 * H * a + rb(r)

    run_steps(
        x, (b0, b1), held, [(ready([got_wa]), wv.at[0], first), (ready([got_wb]), wv.at[1], second)]
    )


def relay(*args):
    return kernel_call(
        relay_body, (STATE, STATE), (VMEM, VMEM), args, [VMEM] * 4 + [ANY] * 4 + [VMEM] * 2, [*SCRATCH, *wbuf(2)], 2,
        16,
    )


def choose_body(ends, made, got, cb1, cb2, out, sem):
    _, x, z, _ = spot()
    load = Load([((x == 0) & (z < 2), ends), ((x == 0) & (z == 2), made), ((x == 0) & (z == 3), got),
                 (x == 1, cb1), (x >= 2, cb2)], out, sem)
    load.start()
    load.wait()


def choose(*args):
    return kernel_call(choose_body, STATE, VMEM, args, [ANY] * 5, [pltpu.SemaphoreType.DMA], 0, 8)


def correct_body(first, ends_in, even_in, ca1, ca2, came, rhs2, rhs3, we2, we3, wa0, wb0, wa1, wb1,
                 fa0, fb0, fa1, fb1, made, got, ends, send, move, coarse, b0, b1, held, xv, xs, wv, ws):
    d, xc, z, _ = spot()
    is_a = z % 2 == 0
    is_b = z % 2 == 1
    odd = z >= 2
    third = z == 3
    other = z != 3
    late = (xc == 3) & odd
    x, ra, g0, g1, rk = (xv.at[n] for n in range(5))
    got_x = Load(
        [((xc == 0) & (z < 2), first), ((xc == 0) & (z == 2), ends_in),
         (((xc == 0) & third) | ((xc > 0) & (z < 2)), even_in),
         ((xc == 1) & odd, ca1), ((xc == 2) & odd, ca2), (late, came)], x, xs.at[0])
    got_e = Load([(third, we3), (other, we2)], wv.at[0], ws.at[0])
    got_ra = Load([(third, rhs3), (other, rhs2)], ra, xs.at[1])
    got_w0 = Load([(is_a, wa0), (is_b, wb0)], wv.at[1], ws.at[1])
    got_w1 = Load([(is_a, wa1.at[0]), (is_b, wb1)], wv.at[2], ws.at[2])
    got_f0 = Load([(is_a, fa0), (is_b, fb0)], g0, xs.at[2])
    got_f1 = Load([(is_a, fa1), (is_b, fb1)], g1, xs.at[3])
    got_r = Load([(is_a, made), (is_b & (d // 4 > 0), got), (is_b & (d // 4 == 0), ends)], rk, xs.at[4])
    start_all(got_x, got_e, got_ra)
    stencil_pads(b0, b1)
    got_x.wait()
    wait_all(got_e, got_ra)
    start_all(got_w0, got_f0, got_r, got_w1, got_f1)

    @pl.when(late)
    def _():
        def update(r, v, a):
            held[r : r + TILE, :] = v + 16 * H * a + ra[r : r + TILE, :]

        run_steps(rows(x), (b0, b1), held, [(nothing, wv.at[0], update)])
        x[...] = held[...]

    def zero(r, v, a):
        rk_rows = rk[r : r + TILE, :]
        coarse[r : r + TILE, :] = jnp.where(d // 4 < 2, rk_rows, v + 16 * H * a + rk_rows)
        value = v + 4 * H * a + g0[r : r + TILE, :]
        move[r : r + TILE, :] = value
        send[r : r + TILE, :] = v
        return value

    def one(r, v, a):
        @pl.when(is_b)
        def _():
            value = v + 4 * H * a + g1[r : r + TILE, :]
            move[r : r + TILE, :] = value
            send[r : r + TILE, :] = value

    run_steps(
        rows(x), (b0, b1), held,
        [(ready([got_w0, got_f0, got_r]), wv.at[1], zero), (ready([got_w1, got_f1]), wv.at[2], one)],
    )


def correct(*args):
    return kernel_call(
        correct_body, (STATE,) * 3, (VMEM,) * 3, args, [ANY] * 12 + [HBM] + [ANY] * 8,
        [*SCRATCH, *room(5), *wbuf(3)], 3, 22
    )


def second_body(x, w2, f2, out, b0, b1, held, wv, ws):
    _, _, z, core = spot()

    @pl.when((core == 1) & (z % 2 == 1))
    def _():
        got = plain(w2, wv.at[0], ws.at[0])
        got.start()
        stencil_pads(b0, b1)
        run_steps(rows(x), (b0, b1), held, [(ready([got]), wv.at[0], coarse_last(f2, out))])


def second(x, w2, f2):
    return kernel_call(second_body, STATE, VMEM, (x, w2, f2), [VMEM, ANY, VMEM], [*SCRATCH, *wbuf(1)], 1, 12)


def finish_body(x0, xa, xb, coarse, w, rhs, out, b0, b1, held, wv, ws, stage, os):
    _, _, z, core = spot()
    is_b = z % 2 == 1
    last = (core == 1) & is_b
    ww = [plain(w.at[n], wv.at[n], ws.at[n]) for n in range(3)]
    start_all(*ww)
    stencil_pads(b0, b1)

    @pl.loop(0, ROWS // TILE)
    def _(i):
        r = pl.multiple_of(i * TILE, TILE)
        at = pl.ds(r, TILE)
        value = jnp.where(core == 0, x0[at, :], jnp.where(is_b, xb[at, :], xa[at, :]))
        held[at, :] = value
        stencil_put(b0, r, value)

    ww[0].wait()
    for r in range(0, ROWS, TILE):
        at = slice(r, r + TILE)
        a = relu_conv(b0, wv.at[0], r)
        v = held[at, :]
        stage[3, at, :] = jnp.where(last, coarse[at, :], v + 4 * H * a + rhs[at, :])
        value = v + H * a
        stage[0, at, :] = value
        stencil_put(b1, r, value)
    pltpu.make_async_copy(stage.at[0], out.at[0], os.at[0]).start()
    pltpu.make_async_copy(stage.at[3], out.at[3], os.at[3]).start()
    for n, source, target in ((1, b1, b0), (2, b0, b1)):
        ww[n].wait()
        for r in range(0, ROWS, TILE):
            at = slice(r, r + TILE)
            value = stage[n - 1, at, :] + H * relu_conv(source, wv.at[n], r)
            stage[n, at, :] = value
            if n == 1:
                stencil_put(target, r, value)
        pltpu.make_async_copy(stage.at[n], out.at[n], os.at[n]).start()
    for n in range(4):
        pltpu.make_async_copy(stage.at[n], out.at[n], os.at[n]).wait()


OUT = jax.ShapeDtypeStruct((4, ROWS, CH), jnp.float32)


def finish(*args):
    return kernel_call(
        finish_body, OUT, ANY, args, [VMEM] * 4 + [HBM, VMEM],
        [*SCRATCH, *wbuf(3), pltpu.VMEM((4, ROWS, CH), jnp.float32), pltpu.SemaphoreType.DMA((4,))], 3, 22,
    )


def widen_body(w, out, wv, sem):
    load = plain(w.at[0], wv, sem)
    load.start()
    load.wait()

    @pl.loop(0, TAPS // TILE)
    def _(n):
        at = pl.ds(pl.multiple_of(n * TILE, TILE), TILE)
        out[at, :] = wv[at, :].astype(jnp.float32)


def widen(w):
    return kernel_call(
        widen_body, jax.ShapeDtypeStruct((TAPS, CH), jnp.float32), VMEM, (w,), [HBM],
        [pltpu.VMEM((TAPS, CH), jnp.bfloat16), pltpu.SemaphoreType.DMA], 0, 8,
    )


def norm_sum_body(a, b, out):
    out[...] = a[...] + b[...]


def norm_sum(a, b):
    return kernel_call(norm_sum_body, jax.ShapeDtypeStruct((8, CH), jnp.float32), VMEM, (a, b), [VMEM, VMEM], [], 0, 2)


def norm_root_body(a, b, out):
    total = jnp.sum(a[...] + b[...])
    root = jnp.sqrt(jnp.full((8, 128), total, jnp.float32) / (4 * ROWS * CH) + 1e-06)
    out[0] = jnp.max(root)


def norm_root(a, b):
    return kernel_call(
        norm_root_body, jax.ShapeDtypeStruct((1,), jnp.float32), pl.BlockSpec(memory_space=pltpu.SMEM), (a, b),
        [VMEM, VMEM], [], 0, 2,
    )


def narrow_body(x, out):
    @pl.loop(0, TAPS // TILE)
    def _(n):
        at = pl.ds(pl.multiple_of(n * TILE, TILE), TILE)
        out[at, :] = x[at, :].astype(jnp.bfloat16)


def narrow(x):
    return kernel_call(narrow_body, jax.ShapeDtypeStruct((TAPS, CH), jnp.bfloat16), VMEM, (x,), [VMEM], [], 0, 8)


PART = TAPS // 4


def pack_body(chip, own, narrowed, out):
    start = lax.axis_index("batch") * PART

    @pl.loop(0, TAPS // TILE)
    def _(n):
        at = pl.ds(pl.multiple_of(n * TILE, TILE), TILE)
        narrowed[at, :] = chip[at, :].astype(jnp.bfloat16)

    @pl.loop(0, PART // 64)
    def _(n):
        at = pl.ds(pl.multiple_of(start + n * 64, 64), 64)
        out[pl.ds(pl.multiple_of(n * 64, 64), 64), :] = chip[at, :]
        out[pl.ds(pl.multiple_of(PART + n * 64, 64), 64), :] = own[at, :]


def pack(chip, own):
    return kernel_call(
        pack_body, (jax.ShapeDtypeStruct((TAPS, CH), jnp.bfloat16), jax.ShapeDtypeStruct((2 * PART, CH), jnp.float32)),
        (VMEM, VMEM), (chip, own), [VMEM, VMEM], [], 0, 8,
    )


def unpack_body(p0, p1, p2, p3, out0, out1):
    y = lax.axis_index("batch")
    for n, part in enumerate((p0, p1, p2, p3)):
        start = (y + 4 - n) % 4 * PART

        @pl.loop(0, PART // 64)
        def _(i, part=part, start=start):
            at = pl.ds(pl.multiple_of(start + i * 64, 64), 64)
            out0[at, :] = part[pl.ds(pl.multiple_of(i * 64, 64), 64), :].astype(jnp.bfloat16)
            out1[at, :] = part[pl.ds(pl.multiple_of(PART + i * 64, 64), 64), :].astype(jnp.bfloat16)


def unpack(*parts):
    kernel = jax.ShapeDtypeStruct((TAPS, CH), jnp.bfloat16)
    return kernel_call(unpack_body, (kernel, kernel), (VMEM, VMEM), parts, [VMEM] * 4, [], 0, 10)


def send(value, pairs, axis="layer"):
    return lax.ppermute(value, axis, pairs)


A0 = [4 * k for k in range(8)]


def cycle(first_state, guess_points, weights):
    first = first_state.reshape(ROWS, CH)
    guess = guess_points.reshape(ROWS, CH)
    w = weights.reshape(4, TAPS, CH)
    shift = [(i, i + 1) for i in range(31)]

    came = send(guess, shift)
    wide = widen(w)
    w_chip = send(wide, [p for k in A0 for p in ((k, k + 1), (k + 2, k + 3))])
    w_z2 = send(wide, [(k + 2, k + 1) for k in A0])
    wn_chip, packed = pack(w_chip, wide)
    part0 = send(packed, [(k + 1, k + 3) for k in A0])
    relaxed = sweep(first, came, w)

    came = send(relaxed, shift)
    w_z3 = send(wide, [(k + 3, k + 1) for k in A0] + [(8 * x, 8 * x + 7) for x in range(1, 4)])
    fine, out0, squares = resweep(first, came, w, relaxed)

    in0 = send(out0, [p for k in A0 for p in ((k, k + 1), (k + 2, k + 3))])
    q1 = one_coarse(in0, w, fine)
    came = send(q1, [(k + 1, k + 3) for k in A0])
    fine_3 = send(fine, [p for k in A0 for p in ((k + 3, k + 1), (k + 1, k + 3))])
    fine_a0 = send(fine, [(k, k + 1) for k in A0])
    ends = two_coarse(came, wn_chip, w, in0, fine)

    ends_in = send(ends, [(k + 3, k + 5) for k in A0[:-1]])
    fine_2 = send(fine, [p for k in A0 for p in ((k + 2, k + 1), (k, k + 3))])
    parts = [part0]
    for n in (1, 2, 3):
        ring = [((k + 3) * 4 + y, (k + 3) * 4 + (y + n) % 4) for k in A0 for y in range(4)]
        parts.append(send(part0, ring, ("layer", "batch")))
    wn_z2, wn_z3 = narrow(w_z2), narrow(w_z3)
    w_even2 = send(w_z3, [(8 * x + 7, 8 * x + 5) for x in range(1, 4)])
    made = group(first, ends_in, wn_chip, w, wn_z2, wn_z3, fine_a0, fine, fine_2, fine_3)

    in_a = send(made, [(5, 13), (9, 15), (17, 23), (25, 31)])
    in_b = send(made, [(5, 15), (9, 13), (17, 21), (25, 29)])
    got = send(made, [(k + 1, k + 3) for k in A0])
    wn_even2 = narrow(w_even2)
    wn_b0, wn_b1 = unpack(*parts)

    common = (in_b, in_a, wn_even2, wn_z3, wn_chip, wn_b0, made, got)
    ca1, cb1 = relay(in_a, in_b, *common)
    came = send(cb1, [(13, 21), (15, 23)])
    swapped = send(squares, [(0, 1), (1, 0), (2, 3), (3, 2)], "batch")
    squares = norm_sum(squares, swapped)
    swapped = send(squares, [(0, 2), (2, 0), (1, 3), (3, 1)], "batch")
    norms = norm_root(squares, swapped)
    ca2, cb2 = relay(came, came, *common)
    came = send(cb2, [(21, 29), (23, 31)])
    carry = choose(ends, made, got, cb1, cb2)
    even_in = send(carry, [(3, 7), (5, 11), (7, 9), (13, 19), (15, 17), (21, 27), (23, 25)])
    out1, move, coarse = correct(
        first, ends_in, even_in, ca1, ca2, came, in_b, in_a, wn_even2, wn_z3, wn_chip, wn_b0, w, wn_b1,
        fine_a0, fine_2, fine, fine_3, made, got, ends,
    )
    in1 = send(out1, [p for k in A0 for p in ((k + 1, k), (k + 3, k + 2))])
    moved = second(move, wn_chip, in0)
    states = finish(in1, move, moved, coarse, w, fine)
    return states.reshape(4, 1, SIDE, SIDE, CH), norms


def solution(mesh):
    placed = (
        P("batch", None, None, None),
        P("layer", "batch", None, None, None),
        P("layer", None, None, None, None),
    )
    return jax.shard_map(
        cycle,
        mesh=mesh,
        in_specs=placed,
        out_specs=(P("layer", "batch", None, None, None), P("layer")),
        check_vma=False,
    )
```

```python
import jax
import jax.numpy as jnp
from jax import lax
from jax.experimental import pallas as pl
from jax.experimental.pallas import tpu as pltpu
from jax.sharding import PartitionSpec as P


CH = 256
SIDE = 32
ROWS = SIDE * SIDE
TAPS = 9 * CH
TILE = 256
H = 2.0 / 128
STATE = jax.ShapeDtypeStruct((ROWS, CH), jnp.float32)
ANY = pl.BlockSpec(memory_space=pl.ANY)
HBM = pl.BlockSpec(memory_space=pltpu.HBM)
VMEM = pl.BlockSpec(memory_space=pltpu.VMEM)


def stencil_put(buf, r, value):
    rows = value.shape[0]
    cube = value.reshape(rows // SIDE, SIDE, CH)
    column = lax.broadcasted_iota(jnp.int32, (1, SIDE, CH), 1)
    before = jnp.where(column == 0, 0.0, pltpu.roll(cube, 1, 1)).reshape(rows, CH)
    behind = jnp.where(column == SIDE - 1, 0.0, pltpu.roll(cube, SIDE - 1, 1)).reshape(rows, CH)
    at = pl.ds(SIDE + r, rows)
    buf[at, 0:CH] = before.astype(jnp.bfloat16)
    buf[at, CH : 2 * CH] = value.astype(jnp.bfloat16)
    buf[at, 2 * CH : 3 * CH] = behind.astype(jnp.bfloat16)


def stencil_pads(*bufs):
    zero = jnp.zeros((SIDE, 3 * CH), jnp.bfloat16)
    for buf in bufs:
        buf[0:SIDE, :] = zero
        buf[SIDE + ROWS :, :] = zero


def relu_conv(buf, weight, r):
    total = None
    for dy in range(3):
        part = jnp.dot(
            buf[pl.ds(r + SIDE * dy, TILE), :],
            weight[pl.ds(3 * CH * dy, 3 * CH), :],
            preferred_element_type=jnp.float32,
        )
        total = part if total is None else total + part
    return jnp.maximum(total, 0.0)


def run_steps(start, bufs, held, steps):
    @pl.loop(0, ROWS // TILE)
    def _(i):
        r = pl.multiple_of(i * TILE, TILE)
        stencil_put(bufs[0], r, start(r))

    for n, (ready, weight, update) in enumerate(steps):
        ready()
        source, target = bufs[n % 2], bufs[(n + 1) % 2]
        for r in range(0, ROWS, TILE):
            current = start(r) if n == 0 else held[r : r + TILE, :]
            value = update(r, current, relu_conv(source, weight, r))
            if n + 1 < len(steps):
                held[r : r + TILE, :] = value
                stencil_put(target, r, value)


def run_pairs(start, bufs, held, copies, weights, update):
    @pl.loop(0, ROWS // TILE)
    def _(i):
        r = pl.multiple_of(i * TILE, TILE)
        value = start(r)
        held[pl.ds(r, TILE), :] = value
        stencil_put(bufs[0], r, value)

    @pl.loop(0, 2)
    def _(turn):
        for slot in range(2):
            copies(2 * turn + slot).wait()
            for r in range(0, ROWS, TILE):
                a = relu_conv(bufs[slot], weights.at[2 * turn + slot], r)
                value = update(turn, slot, r, held[r : r + TILE, :], a)
                held[r : r + TILE, :] = value
                stencil_put(bufs[1 - slot], r, value)


SCRATCH = (
    pltpu.VMEM((ROWS + 2 * SIDE, 3 * CH), jnp.bfloat16),
    pltpu.VMEM((ROWS + 2 * SIDE, 3 * CH), jnp.bfloat16),
    pltpu.VMEM((ROWS, CH), jnp.float32),
)


class Load:
    def __init__(self, choices, target, sem):
        self.choices, self.target, self.sem = choices, target, sem

    def start(self):
        for condition, source in self.choices:
            if condition is None:
                pltpu.make_async_copy(source, self.target, self.sem).start()
                continue

            @pl.when(condition)
            def _(source=source):
                pltpu.make_async_copy(source, self.target, self.sem).start()

    def wait(self):
        pltpu.make_async_copy(self.choices[0][1], self.target, self.sem).wait()


def plain(source, target, sem):
    return Load([(None, source)], target, sem)


def start_all(*loads):
    for load in loads:
        load.start()


def wait_all(*loads):
    for load in loads:
        load.wait()


def rows(ref):
    return lambda r: ref[pl.ds(r, TILE), :]


def either(condition, yes, no):
    return lambda r: jnp.where(condition, yes[pl.ds(r, TILE), :], no[pl.ds(r, TILE), :])


def ready(waits, starts=()):
    def run():
        wait_all(*waits)
        start_all(*starts)

    return run


def spot():
    d = lax.axis_index("layer")
    return d, d // 8, (d // 2) % 4, d % 2


def nothing():
    return None


def kernel_call(body, outs, out_specs, args, in_specs, scratch, convs, grant, aliases=None):
    return pl.pallas_call(
        body,
        out_shape=outs,
        in_specs=in_specs,
        out_specs=out_specs,
        scratch_shapes=scratch,
        input_output_aliases=aliases or {},
        compiler_params=pltpu.CompilerParams(vmem_limit_bytes=grant << 20),
        cost_estimate=pl.CostEstimate(flops=convs * 2 * ROWS * TAPS * CH, bytes_accessed=4 << 20, transcendentals=0),
    )(*args)


def room(n):
    return [pltpu.VMEM((n, ROWS, CH), jnp.float32), pltpu.SemaphoreType.DMA((n,))]


def wbuf(n):
    return [pltpu.VMEM((n, TAPS, CH), jnp.bfloat16), pltpu.SemaphoreType.DMA((n,))]


def sweep_body(first, given, w, out, b0, b1, wv, ws):
    x = either(lax.axis_index("layer") == 0, first, given)

    def copies(n):
        return pltpu.make_async_copy(w.at[n], wv.at[n], ws.at[n])

    start_all(*(copies(n) for n in range(4)))
    stencil_pads(b0, b1)
    run_pairs(x, (b0, b1), out, copies, wv, lambda turn, slot, r, v, a: v + H * a)


def sweep(first, given, w):
    return kernel_call(sweep_body, STATE, VMEM, (first, given, w), [VMEM, VMEM, HBM], [*SCRATCH[:2], *wbuf(4)], 4, 16)


def resweep_body(first, given, w, relaxed, fine, send, squares, b0, b1, held, ahead, sums, wv, ws):
    d = lax.axis_index("layer")
    x = either(d == 0, first, given)

    def copies(n):
        return pltpu.make_async_copy(w.at[n], wv.at[n], ws.at[n])

    start_all(*(copies(n) for n in range(4)))
    stencil_pads(b0, b1)
    sums[...] = jnp.zeros_like(sums)

    def update(turn, slot, r, v, a):
        value = v + H * a
        at = slice(r, r + TILE)
        if slot == 0:
            ahead[turn, at, :] = v + 4 * H * a
            return value
        rhs = value - ahead[0, at, :]
        fine[at, :] = rhs
        off = value - relaxed[at, :]
        sums[turn] += jnp.sum((off * off).reshape(TILE // 8, 8, CH), axis=0)
        send[at, :] = jnp.where(d % 4 < 2, value, rhs)
        return value

    run_pairs(x, (b0, b1), held, copies, wv, update)
    squares[...] = sums[1]


def resweep(first, given, w, relaxed):
    return kernel_call(
        resweep_body, (STATE, STATE, jax.ShapeDtypeStruct((8, CH), jnp.float32)), (VMEM,) * 3,
        (first, given, w, relaxed), [VMEM, VMEM, HBM, VMEM],
        [*SCRATCH, pltpu.VMEM((2, ROWS, CH), jnp.float32), pltpu.VMEM((2, 8, CH), jnp.float32), *wbuf(4)], 4,
        20,
    )


def coarse_update(rhs):
    return lambda r, v, a: v + 4 * H * a + rhs[r : r + TILE, :]


def coarse_last(rhs, out):
    def update(r, v, a):
        out[r : r + TILE, :] = v + 4 * H * a + rhs[r : r + TILE, :]

    return update


def one_coarse_body(x, w, rhs, out, b0, b1, held, fv, fs, wv, ws):
    ww = plain(w.at[0], wv.at[0], ws.at[0])
    ff = plain(rhs, fv.at[0], fs.at[0])
    start_all(ww, ff)
    stencil_pads(b0, b1)
    run_steps(rows(x), (b0, b1), held, [(ready([ww, ff]), wv.at[0], coarse_last(fv.at[0], out))])


def one_coarse(x, w, rhs):
    return kernel_call(
        one_coarse_body, STATE, VMEM, (x, w, rhs), [VMEM, HBM, ANY], [*SCRATCH, *room(1), *wbuf(1)], 1,
        14,
    )


def two_coarse_body(x, wa, w, rhs_a, rhs_b, out, b0, b1, held, fv, fs, wv, ws):
    ww = [plain(wa, wv.at[0], ws.at[0]), plain(w.at[0], wv.at[1], ws.at[1])]
    ff = [plain(rhs_a, fv.at[0], fs.at[0]), plain(rhs_b, fv.at[1], fs.at[1])]
    start_all(ww[0], ff[0])
    stencil_pads(b0, b1)
    run_steps(
        rows(x), (b0, b1), held,
        [(ready([ww[0], ff[0]], [ww[1], ff[1]]), wv.at[0], coarse_update(fv.at[0])),
         (ready([ww[1], ff[1]]), wv.at[1], coarse_last(fv.at[1], out))],
    )


def two_coarse(x, wa, w, rhs_a, rhs_b):
    return kernel_call(
        two_coarse_body, STATE, VMEM, (x, wa, w, rhs_a, rhs_b), [VMEM, ANY, HBM, ANY, ANY],
        [*SCRATCH, *room(2), *wbuf(2)], 2, 16,
    )


def group_body(first, ends, w0, w1, w2, w3, f0, f1, f2, f3, out, b0, b1, held, ahead, fv, fs, wv, ws):
    d = lax.axis_index("layer")
    x = either(d == 1, first, ends)
    ww = [plain(s, wv.at[n], ws.at[n]) for n, s in enumerate((w0, w1.at[0], w2, w3))]
    ff = [plain(s, fv.at[n], fs.at[n]) for n, s in enumerate((f0, f1, f2, f3))]
    for n in range(4):
        start_all(ww[n], ff[n])
    stencil_pads(b0, b1)

    class copies:
        def __init__(self, n):
            self.n = n

        def wait(self):
            pltpu.make_async_copy(w0, wv.at[self.n], ws.at[self.n]).wait()
            pltpu.make_async_copy(f0, fv.at[self.n], fs.at[self.n]).wait()

    def update(turn, slot, r, v, a):
        at = slice(r, r + TILE)
        value = v + 4 * H * a + fv[2 * turn + slot, at, :]
        if slot == 0:
            ahead[turn, at, :] = v + 16 * H * a
        else:
            out[at, :] = jnp.where(d == 5, value, value - ahead[0, at, :])
        return value

    run_pairs(x, (b0, b1), held, copies, wv, update)


def group(*args):
    return kernel_call(
        group_body, STATE, VMEM, args, [VMEM, VMEM, ANY, HBM] + [ANY] * 6,
        [*SCRATCH, pltpu.VMEM((2, ROWS, CH), jnp.float32), *room(4), *wbuf(4)], 4, 22,
    )


def relay_body(came2, came3, rhs2, rhs3, we2, we3, w02, w03, own2, own3, ca, cb, b0, b1, held, wv, ws):
    _, _, z, _ = spot()
    third = z == 3
    other = z != 3
    x, ra, rb = either(third, came3, came2), either(third, rhs3, rhs2), either(third, own3, own2)
    got_wa = Load([(third, we3), (other, we2)], wv.at[0], ws.at[0])
    got_wb = Load([(third, w03), (other, w02)], wv.at[1], ws.at[1])
    start_all(got_wa, got_wb)
    stencil_pads(b0, b1)

    def first(r, v, a):
        value = v + 16 * H * a + ra(r)
        ca[r : r + TILE, :] = value
        return value

    def second(r, v, a):
        cb[r : r + TILE, :] = v + 16 * H * a + rb(r)

    run_steps(
        x, (b0, b1), held, [(ready([got_wa]), wv.at[0], first), (ready([got_wb]), wv.at[1], second)]
    )


def relay(*args):
    return kernel_call(
        relay_body, (STATE, STATE), (VMEM, VMEM), args, [VMEM] * 4 + [ANY] * 4 + [VMEM] * 2, [*SCRATCH, *wbuf(2)], 2,
        16,
    )


def choose_body(ends, made, got, cb1, cb2, out, sem):
    _, x, z, _ = spot()
    load = Load([((x == 0) & (z < 2), ends), ((x == 0) & (z == 2), made), ((x == 0) & (z == 3), got),
                 (x == 1, cb1), (x >= 2, cb2)], out, sem)
    load.start()
    load.wait()


def choose(*args):
    return kernel_call(choose_body, STATE, VMEM, args, [ANY] * 5, [pltpu.SemaphoreType.DMA], 0, 8)


def correct_body(first, ends_in, even_in, even2_in, ca1, ca2, came, rhs2, rhs3, we2, we3, wa0, wb0, wa1, wb1,
                 fa0, fb0, fa1, fb1, made, got3, got1, ends, send, move, coarse, b0, b1, held, xv, xs, wv, ws):
    d, xc, z, _ = spot()
    is_a = z % 2 == 0
    is_b = z % 2 == 1
    odd = z >= 2
    third = z == 3
    other = z != 3
    late = (xc == 3) & odd
    x, ra, g0, g1, rk = (xv.at[n] for n in range(5))
    got_x = Load(
        [((xc == 0) & (z < 2), first), ((xc == 0) & (z == 2), ends_in),
         (((xc == 0) & third) | ((xc > 0) & (z < 2) & (d != 25)), even_in), (d == 25, even2_in),
         ((xc == 1) & odd, ca1), ((xc == 2) & odd, ca2), (late, came)], x, xs.at[0])
    got_e = Load([(third, we3), (other, we2)], wv.at[0], ws.at[0])
    got_ra = Load([(third, rhs3), (other, rhs2)], ra, xs.at[1])
    got_w0 = Load([(is_a, wa0), (is_b, wb0)], wv.at[1], ws.at[1])
    got_w1 = Load([(is_a, wa1.at[0]), (is_b, wb1)], wv.at[2], ws.at[2])
    got_f0 = Load([(is_a, fa0), (is_b, fb0)], g0, xs.at[2])
    got_f1 = Load([(is_a, fa1), (is_b, fb1)], g1, xs.at[3])
    got_r = Load(
        [(is_a, made), (third, got3), ((z == 1) & (d // 4 > 0), got1), ((z == 1) & (d // 4 == 0), ends)],
        rk, xs.at[4])
    start_all(got_x, got_e, got_ra)
    stencil_pads(b0, b1)
    got_x.wait()
    wait_all(got_e, got_ra)
    start_all(got_w0, got_f0, got_r, got_w1, got_f1)

    @pl.when(late)
    def _():
        def update(r, v, a):
            held[r : r + TILE, :] = v + 16 * H * a + ra[r : r + TILE, :]

        run_steps(rows(x), (b0, b1), held, [(nothing, wv.at[0], update)])
        x[...] = held[...]

    def zero(r, v, a):
        rk_rows = rk[r : r + TILE, :]
        coarse[r : r + TILE, :] = jnp.where(d // 4 < 2, rk_rows, v + 16 * H * a + rk_rows)
        value = v + 4 * H * a + g0[r : r + TILE, :]
        move[r : r + TILE, :] = value
        send[r : r + TILE, :] = v
        stencil_put(b1, r, value)

    run_steps(rows(x), (b0, b1), held, [(ready([got_w0, got_f0, got_r]), wv.at[1], zero)])
    wait_all(got_w1, got_f1)

    @pl.when(is_b)
    def _():
        for r in range(0, ROWS, TILE):
            at = slice(r, r + TILE)
            value = move[at, :] + 4 * H * relu_conv(b1, wv.at[2], r) + g1[at, :]
            move[at, :] = value
            send[at, :] = value


def correct(*args):
    return kernel_call(
        correct_body, (STATE,) * 3, (VMEM,) * 3, args, [ANY] * 13 + [HBM] + [ANY] * 9,
        [*SCRATCH, *room(5), *wbuf(3)], 3, 22
    )


def second_body(x, w2, f2, out, b0, b1, held, wv, ws):
    _, _, z, core = spot()

    @pl.when((core == 1) & (z % 2 == 1))
    def _():
        got = plain(w2, wv.at[0], ws.at[0])
        got.start()
        stencil_pads(b0, b1)
        run_steps(rows(x), (b0, b1), held, [(ready([got]), wv.at[0], coarse_last(f2, out))])


def second(x, w2, f2):
    return kernel_call(second_body, STATE, VMEM, (x, w2, f2), [VMEM, ANY, VMEM], [*SCRATCH, *wbuf(1)], 1, 12)


def finish_body(x0, xa, xb, coarse, w, rhs, out, b0, b1, held, wv, ws, stage, os):
    _, _, z, core = spot()
    is_b = z % 2 == 1
    last = (core == 1) & is_b
    ww = [plain(w.at[n], wv.at[n], ws.at[n]) for n in range(3)]
    start_all(*ww)
    stencil_pads(b0, b1)

    @pl.loop(0, ROWS // TILE)
    def _(i):
        r = pl.multiple_of(i * TILE, TILE)
        at = pl.ds(r, TILE)
        value = jnp.where(core == 0, x0[at, :], jnp.where(is_b, xb[at, :], xa[at, :]))
        held[at, :] = value
        stencil_put(b0, r, value)

    ww[0].wait()
    for r in range(0, ROWS, TILE):
        at = slice(r, r + TILE)
        a = relu_conv(b0, wv.at[0], r)
        v = held[at, :]
        stage[3, at, :] = jnp.where(last, coarse[at, :], v + 4 * H * a + rhs[at, :])
        value = v + H * a
        stage[0, at, :] = value
        stencil_put(b1, r, value)
    pltpu.make_async_copy(stage.at[0], out.at[0], os.at[0]).start()
    pltpu.make_async_copy(stage.at[3], out.at[3], os.at[3]).start()
    for n, source, target in ((1, b1, b0), (2, b0, b1)):
        ww[n].wait()
        for r in range(0, ROWS, TILE):
            at = slice(r, r + TILE)
            value = stage[n - 1, at, :] + H * relu_conv(source, wv.at[n], r)
            stage[n, at, :] = value
            if n == 1:
                stencil_put(target, r, value)
        pltpu.make_async_copy(stage.at[n], out.at[n], os.at[n]).start()
    for n in range(4):
        pltpu.make_async_copy(stage.at[n], out.at[n], os.at[n]).wait()


OUT = jax.ShapeDtypeStruct((4, ROWS, CH), jnp.float32)


def finish(*args):
    return kernel_call(
        finish_body, OUT, ANY, args, [VMEM] * 4 + [HBM, VMEM],
        [*SCRATCH, *wbuf(3), pltpu.VMEM((4, ROWS, CH), jnp.float32), pltpu.SemaphoreType.DMA((4,))], 3, 22,
    )


def widen_body(w, out, wv, sem):
    load = plain(w.at[0], wv, sem)
    load.start()
    load.wait()

    @pl.loop(0, TAPS // TILE)
    def _(n):
        at = pl.ds(pl.multiple_of(n * TILE, TILE), TILE)
        out[at, :] = wv[at, :].astype(jnp.float32)


def widen(w):
    return kernel_call(
        widen_body, jax.ShapeDtypeStruct((TAPS, CH), jnp.float32), VMEM, (w,), [HBM],
        [pltpu.VMEM((TAPS, CH), jnp.bfloat16), pltpu.SemaphoreType.DMA], 0, 8,
    )


def norm_sum_body(a, b, out):
    out[...] = a[...] + b[...]


def norm_sum(a, b):
    return kernel_call(norm_sum_body, jax.ShapeDtypeStruct((8, CH), jnp.float32), VMEM, (a, b), [VMEM, VMEM], [], 0, 2)


def norm_root_body(a, b, out):
    total = jnp.sum(a[...] + b[...])
    root = jnp.sqrt(jnp.full((8, 128), total, jnp.float32) / (4 * ROWS * CH) + 1e-06)
    out[0] = jnp.max(root)


def norm_root(a, b):
    return kernel_call(
        norm_root_body, jax.ShapeDtypeStruct((1,), jnp.float32), pl.BlockSpec(memory_space=pltpu.SMEM), (a, b),
        [VMEM, VMEM], [], 0, 2,
    )


def narrow_body(x, out):
    @pl.loop(0, TAPS // TILE)
    def _(n):
        at = pl.ds(pl.multiple_of(n * TILE, TILE), TILE)
        out[at, :] = x[at, :].astype(jnp.bfloat16)


def narrow(x):
    return kernel_call(narrow_body, jax.ShapeDtypeStruct((TAPS, CH), jnp.bfloat16), VMEM, (x,), [VMEM], [], 0, 8)


PART = TAPS // 4


def pack_body(chip, own, narrowed, out):
    start = lax.axis_index("batch") * PART

    @pl.loop(0, TAPS // TILE)
    def _(n):
        at = pl.ds(pl.multiple_of(n * TILE, TILE), TILE)
        narrowed[at, :] = chip[at, :].astype(jnp.bfloat16)

    @pl.loop(0, PART // 64)
    def _(n):
        at = pl.ds(pl.multiple_of(start + n * 64, 64), 64)
        out[pl.ds(pl.multiple_of(n * 64, 64), 64), :] = chip[at, :]
        out[pl.ds(pl.multiple_of(PART + n * 64, 64), 64), :] = own[at, :]


def pack(chip, own):
    return kernel_call(
        pack_body, (jax.ShapeDtypeStruct((TAPS, CH), jnp.bfloat16), jax.ShapeDtypeStruct((2 * PART, CH), jnp.float32)),
        (VMEM, VMEM), (chip, own), [VMEM, VMEM], [], 0, 8,
    )


def unpack_body(p0, p1, p2, p3, out0, out1):
    y = lax.axis_index("batch")
    for n, part in enumerate((p0, p1, p2, p3)):
        start = (y + 4 - n) % 4 * PART

        @pl.loop(0, PART // 64)
        def _(i, part=part, start=start):
            at = pl.ds(pl.multiple_of(start + i * 64, 64), 64)
            out0[at, :] = part[pl.ds(pl.multiple_of(i * 64, 64), 64), :].astype(jnp.bfloat16)
            out1[at, :] = part[pl.ds(pl.multiple_of(PART + i * 64, 64), 64), :].astype(jnp.bfloat16)


def unpack(*parts):
    kernel = jax.ShapeDtypeStruct((TAPS, CH), jnp.bfloat16)
    return kernel_call(unpack_body, (kernel, kernel), (VMEM, VMEM), parts, [VMEM] * 4, [], 0, 10)


def send(value, pairs, axis="layer"):
    return lax.ppermute(value, axis, pairs)


A0 = [4 * k for k in range(8)]


def cycle(first_state, guess_points, weights):
    first = first_state.reshape(ROWS, CH)
    guess = guess_points.reshape(ROWS, CH)
    w = weights.reshape(4, TAPS, CH)
    shift = [(i, i + 1) for i in range(31)]

    came = send(guess, shift)
    wide = widen(w)
    w_chip = send(wide, [p for k in A0 for p in ((k, k + 1), (k + 2, k + 3))])
    w_z2 = send(wide, [(k + 2, k + 1) for k in A0])
    wn_chip, packed = pack(w_chip, wide)
    part0 = send(packed, [(k + 1, k + 3) for k in A0])
    relaxed = sweep(first, came, w)

    came = send(relaxed, shift)
    w_z3 = send(wide, [(k + 3, k + 1) for k in A0] + [(8 * x, 8 * x + 7) for x in range(1, 4)])
    fine, out0, squares = resweep(first, came, w, relaxed)

    in0 = send(out0, [p for k in A0 for p in ((k, k + 1), (k + 2, k + 3))])
    q1 = one_coarse(in0, w, fine)
    came = send(q1, [(k + 1, k + 3) for k in A0])
    fine_3 = send(fine, [p for k in A0 for p in ((k + 3, k + 1), (k + 1, k + 3))])
    fine_a0 = send(fine, [(k, k + 1) for k in A0])
    ends = two_coarse(came, wn_chip, w, in0, fine)

    ends_in = send(ends, [(k + 3, k + 5) for k in A0[:-1]])
    fine_2 = send(fine, [p for k in A0 for p in ((k + 2, k + 1), (k, k + 3))])
    parts = [part0]
    for n in (1, 2, 3):
        ring = [((k + 3) * 4 + y, (k + 3) * 4 + (y + n) % 4) for k in A0 for y in range(4)]
        parts.append(send(part0, ring, ("layer", "batch")))
    wn_z2, wn_z3 = narrow(w_z2), narrow(w_z3)
    w_even2 = send(w_z3, [(8 * x + 7, 8 * x + 5) for x in range(1, 4)])
    made = group(first, ends_in, wn_chip, w, wn_z2, wn_z3, fine_a0, fine, fine_2, fine_3)

    in_c = send(made, [(9, 13), (17, 21), (25, 29), (5, 7), (13, 15), (21, 23), (29, 31)])
    in_a = send(made, [(5, 13), (9, 15), (17, 23), (25, 31)])
    in_d = send(made, [(5, 15), (1, 3), (9, 11), (17, 19), (25, 27)])
    wn_even2 = narrow(w_even2)
    wn_b0, wn_b1 = unpack(*parts)

    common = (in_c, in_a, wn_even2, wn_z3, wn_chip, wn_b0, made, in_c)
    ca1, cb1 = relay(in_a, in_d, *common)
    came = send(cb1, [(13, 21), (15, 23)])
    swapped = send(squares, [(0, 1), (1, 0), (2, 3), (3, 2)], "batch")
    squares = norm_sum(squares, swapped)
    swapped = send(squares, [(0, 2), (2, 0), (1, 3), (3, 1)], "batch")
    norms = norm_root(squares, swapped)
    ca2, cb2 = relay(came, came, *common)
    came = send(cb2, [(21, 29), (23, 31)])
    carry = choose(ends, made, in_c, cb1, cb2)
    even_in = send(carry, [(3, 7), (5, 11), (7, 9), (13, 19), (15, 17), (21, 27)])
    even2_in = send(came, [(29, 25)])
    out1, move, coarse = correct(
        first, ends_in, even_in, even2_in, ca1, ca2, came, in_c, in_a, wn_even2, wn_z3, wn_chip, wn_b0, w, wn_b1,
        fine_a0, fine_2, fine, fine_3, made, in_c, in_d, ends,
    )
    in1 = send(out1, [p for k in A0 for p in ((k + 1, k), (k + 3, k + 2))])
    moved = second(move, wn_chip, in0)
    states = finish(in1, move, moved, coarse, w, fine)
    return states.reshape(4, 1, SIDE, SIDE, CH), norms


def solution(mesh):
    placed = (
        P("batch", None, None, None),
        P("layer", "batch", None, None, None),
        P("layer", None, None, None, None),
    )
    return jax.shard_map(
        cycle,
        mesh=mesh,
        in_specs=placed,
        out_specs=(P("layer", "batch", None, None, None), P("layer")),
        check_vma=False,
    )
```

```python
import jax
import jax.numpy as jnp
from jax import lax
from jax.experimental import pallas as pl
from jax.experimental.pallas import tpu as pltpu
from jax.sharding import PartitionSpec as P


(WIDEN, PACK, SWEEP, RESWEEP, ONE, TWO, NARROW_2, NARROW_3, GROUP, UNPACK, NARROW_E, RELAY1, NORM_SUM, NORM_ROOT, RELAY2,
 CHOOSE, CORRECT, SECOND, FINISH) = range(100, 119)

CH = 256
SIDE = 32
ROWS = SIDE * SIDE
TAPS = 9 * CH
TILE = 256
H = 2.0 / 128
STATE = jax.ShapeDtypeStruct((ROWS, CH), jnp.float32)
ANY = pl.BlockSpec(memory_space=pl.ANY)
HBM = pl.BlockSpec(memory_space=pltpu.HBM)
VMEM = pl.BlockSpec(memory_space=pltpu.VMEM)


def stencil_put(buf, r, value):
    rows = value.shape[0]
    cube = value.reshape(rows // SIDE, SIDE, CH)
    column = lax.broadcasted_iota(jnp.int32, (1, SIDE, CH), 1)
    before = jnp.where(column == 0, 0.0, pltpu.roll(cube, 1, 1)).reshape(rows, CH)
    behind = jnp.where(column == SIDE - 1, 0.0, pltpu.roll(cube, SIDE - 1, 1)).reshape(rows, CH)
    at = pl.ds(SIDE + r, rows)
    buf[at, 0:CH] = before.astype(jnp.bfloat16)
    buf[at, CH : 2 * CH] = value.astype(jnp.bfloat16)
    buf[at, 2 * CH : 3 * CH] = behind.astype(jnp.bfloat16)


def stencil_pads(*bufs):
    zero = jnp.zeros((SIDE, 3 * CH), jnp.bfloat16)
    for buf in bufs:
        buf[0:SIDE, :] = zero
        buf[SIDE + ROWS :, :] = zero


def relu_conv(buf, weight, r):
    total = None
    for dy in range(3):
        part = jnp.dot(
            buf[pl.ds(r + SIDE * dy, TILE), :],
            weight[pl.ds(3 * CH * dy, 3 * CH), :],
            preferred_element_type=jnp.float32,
        )
        total = part if total is None else total + part
    return jnp.maximum(total, 0.0)


def run_steps(start, bufs, held, steps):
    @pl.loop(0, ROWS // TILE)
    def _(i):
        r = pl.multiple_of(i * TILE, TILE)
        stencil_put(bufs[0], r, start(r))

    for n, (ready, weight, update) in enumerate(steps):
        ready()
        source, target = bufs[n % 2], bufs[(n + 1) % 2]
        for r in range(0, ROWS, TILE):
            current = start(r) if n == 0 else held[r : r + TILE, :]
            value = update(r, current, relu_conv(source, weight, r))
            if n + 1 < len(steps):
                held[r : r + TILE, :] = value
                stencil_put(target, r, value)


def run_pairs(start, bufs, held, copies, weights, update):
    @pl.loop(0, ROWS // TILE)
    def _(i):
        r = pl.multiple_of(i * TILE, TILE)
        value = start(r)
        held[pl.ds(r, TILE), :] = value
        stencil_put(bufs[0], r, value)

    @pl.loop(0, 2)
    def _(turn):
        for slot in range(2):
            copies(2 * turn + slot).wait()
            for r in range(0, ROWS, TILE):
                a = relu_conv(bufs[slot], weights.at[2 * turn + slot], r)
                value = update(turn, slot, r, held[r : r + TILE, :], a)
                held[r : r + TILE, :] = value
                stencil_put(bufs[1 - slot], r, value)


SCRATCH = (
    pltpu.VMEM((ROWS + 2 * SIDE, 3 * CH), jnp.bfloat16),
    pltpu.VMEM((ROWS + 2 * SIDE, 3 * CH), jnp.bfloat16),
    pltpu.VMEM((ROWS, CH), jnp.float32),
)


class Load:
    def __init__(self, choices, target, sem):
        self.choices, self.target, self.sem = choices, target, sem

    def start(self):
        for condition, source in self.choices:
            if condition is None:
                pltpu.make_async_copy(source, self.target, self.sem).start()
                continue

            @pl.when(condition)
            def _(source=source):
                pltpu.make_async_copy(source, self.target, self.sem).start()

    def wait(self):
        pltpu.make_async_copy(self.choices[0][1], self.target, self.sem).wait()


def plain(source, target, sem):
    return Load([(None, source)], target, sem)


def start_all(*loads):
    for load in loads:
        load.start()


def wait_all(*loads):
    for load in loads:
        load.wait()


def rows(ref):
    return lambda r: ref[pl.ds(r, TILE), :]


def either(condition, yes, no):
    return lambda r: jnp.where(condition, yes[pl.ds(r, TILE), :], no[pl.ds(r, TILE), :])


def ready(waits, starts=()):
    def run():
        wait_all(*waits)
        start_all(*starts)

    return run


def spot():
    d = lax.axis_index("layer")
    return d, d // 8, (d // 2) % 4, d % 2


def nothing():
    return None


def roles():
    _, _, z, core = spot()
    one = core == 1
    return {ONE: one & (z % 2 == 0), TWO: one & (z % 2 == 1), GROUP: one & (z % 2 == 0), RELAY1: one & (z >= 2),
            RELAY2: one & (z >= 2), CORRECT: one}


def guarded(body, name):
    def run(*refs):
        @pl.when(roles()[name])
        def _():
            body(*refs)

    return run if name in (ONE, TWO, GROUP, RELAY1, RELAY2, CORRECT) else body


def kernel_call(body, outs, out_specs, args, in_specs, scratch, convs, name, grant, aliases=None):
    return pl.pallas_call(
        guarded(body, name),
        out_shape=outs,
        in_specs=in_specs,
        out_specs=out_specs,
        scratch_shapes=scratch,
        input_output_aliases=aliases or {},
        compiler_params=pltpu.CompilerParams(vmem_limit_bytes=grant << 20),
        cost_estimate=pl.CostEstimate(flops=convs * 2 * ROWS * TAPS * CH, bytes_accessed=4 << 20, transcendentals=0),
    )(*args)


def room(n):
    return [pltpu.VMEM((n, ROWS, CH), jnp.float32), pltpu.SemaphoreType.DMA((n,))]


def wbuf(n):
    return [pltpu.VMEM((n, TAPS, CH), jnp.bfloat16), pltpu.SemaphoreType.DMA((n,))]


def sweep_body(first, given, w, out, b0, b1, wv, ws):
    x = either(lax.axis_index("layer") == 0, first, given)

    def copies(n):
        return pltpu.make_async_copy(w.at[n], wv.at[n], ws.at[n])

    start_all(*(copies(n) for n in range(4)))
    stencil_pads(b0, b1)
    run_pairs(x, (b0, b1), out, copies, wv, lambda turn, slot, r, v, a: v + H * a)


def sweep(first, given, w):
    return kernel_call(
        sweep_body, STATE, VMEM, (first, given, w), [VMEM, VMEM, HBM], [*SCRATCH[:2], *wbuf(4)], 4, SWEEP, 16
    )


def resweep_body(first, given, w, relaxed, fine, send, squares, b0, b1, held, ahead, sums, wv, ws):
    d = lax.axis_index("layer")
    x = either(d == 0, first, given)

    def copies(n):
        return pltpu.make_async_copy(w.at[n], wv.at[n], ws.at[n])

    start_all(*(copies(n) for n in range(4)))
    stencil_pads(b0, b1)
    sums[...] = jnp.zeros_like(sums)

    def update(turn, slot, r, v, a):
        value = v + H * a
        at = slice(r, r + TILE)
        if slot == 0:
            ahead[turn, at, :] = v + 4 * H * a
            return value
        rhs = value - ahead[0, at, :]
        fine[at, :] = rhs
        off = value - relaxed[at, :]
        sums[turn] += jnp.sum((off * off).reshape(TILE // 8, 8, CH), axis=0)
        send[at, :] = jnp.where(d % 4 < 2, value, rhs)
        return value

    run_pairs(x, (b0, b1), held, copies, wv, update)
    squares[...] = sums[1]


def resweep(first, given, w, relaxed):
    return kernel_call(
        resweep_body, (STATE, STATE, jax.ShapeDtypeStruct((8, CH), jnp.float32)), (VMEM,) * 3,
        (first, given, w, relaxed), [VMEM, VMEM, HBM, VMEM],
        [*SCRATCH, pltpu.VMEM((2, ROWS, CH), jnp.float32), pltpu.VMEM((2, 8, CH), jnp.float32), *wbuf(4)], 4,
        RESWEEP, 20,
    )


def coarse_update(rhs):
    return lambda r, v, a: v + 4 * H * a + rhs[r : r + TILE, :]


def coarse_last(rhs, out):
    def update(r, v, a):
        out[r : r + TILE, :] = v + 4 * H * a + rhs[r : r + TILE, :]

    return update


def one_coarse_body(x, w, rhs, out, b0, b1, held, fv, fs, wv, ws):
    ww = plain(w.at[0], wv.at[0], ws.at[0])
    ff = plain(rhs, fv.at[0], fs.at[0])
    start_all(ww, ff)
    stencil_pads(b0, b1)
    run_steps(rows(x), (b0, b1), held, [(ready([ww, ff]), wv.at[0], coarse_last(fv.at[0], out))])


def one_coarse(x, w, rhs):
    return kernel_call(
        one_coarse_body, STATE, VMEM, (x, w, rhs), [VMEM, HBM, ANY], [*SCRATCH, *room(1), *wbuf(1)], 1,
        ONE, 14,
    )


def two_coarse_body(x, wa, w, rhs_a, rhs_b, out, b0, b1, held, fv, fs, wv, ws):
    ww = [plain(wa, wv.at[0], ws.at[0]), plain(w.at[0], wv.at[1], ws.at[1])]
    ff = [plain(rhs_a, fv.at[0], fs.at[0]), plain(rhs_b, fv.at[1], fs.at[1])]
    start_all(ww[0], ff[0])
    stencil_pads(b0, b1)
    run_steps(
        rows(x), (b0, b1), held,
        [(ready([ww[0], ff[0]], [ww[1], ff[1]]), wv.at[0], coarse_update(fv.at[0])),
         (ready([ww[1], ff[1]]), wv.at[1], coarse_last(fv.at[1], out))],
    )


def two_coarse(x, wa, w, rhs_a, rhs_b):
    return kernel_call(
        two_coarse_body, STATE, VMEM, (x, wa, w, rhs_a, rhs_b), [VMEM, ANY, HBM, ANY, ANY],
        [*SCRATCH, *room(2), *wbuf(2)], 2, TWO, 16,
    )


def group_body(first, ends, w0, w1, w2, w3, f0, f1, f2, f3, out, b0, b1, held, ahead, fv, fs, wv, ws):
    d = lax.axis_index("layer")
    x = either(d == 1, first, ends)
    ww = [plain(s, wv.at[n], ws.at[n]) for n, s in enumerate((w0, w1.at[0], w2, w3))]
    ff = [plain(s, fv.at[n], fs.at[n]) for n, s in enumerate((f0, f1, f2, f3))]
    for n in range(4):
        start_all(ww[n], ff[n])
    stencil_pads(b0, b1)

    class copies:
        def __init__(self, n):
            self.n = n

        def wait(self):
            pltpu.make_async_copy(w0, wv.at[self.n], ws.at[self.n]).wait()
            pltpu.make_async_copy(f0, fv.at[self.n], fs.at[self.n]).wait()

    def update(turn, slot, r, v, a):
        at = slice(r, r + TILE)
        value = v + 4 * H * a + fv[2 * turn + slot, at, :]
        if slot == 0:
            ahead[turn, at, :] = v + 16 * H * a
        else:
            out[at, :] = jnp.where(d == 5, value, value - ahead[0, at, :])
        return value

    run_pairs(x, (b0, b1), held, copies, wv, update)


def group(*args):
    return kernel_call(
        group_body, STATE, VMEM, args, [VMEM, VMEM, ANY, HBM] + [ANY] * 6,
        [*SCRATCH, pltpu.VMEM((2, ROWS, CH), jnp.float32), *room(4), *wbuf(4)], 4, GROUP, 22,
    )


def relay_body(came2, came3, rhs2, rhs3, we2, we3, w02, w03, own2, own3, ca, cb, b0, b1, held, wv, ws):
    _, _, z, _ = spot()
    third = z == 3
    other = z != 3
    x, ra, rb = either(third, came3, came2), either(third, rhs3, rhs2), either(third, own3, own2)
    got_wa = Load([(third, we3), (other, we2)], wv.at[0], ws.at[0])
    got_wb = Load([(third, w03), (other, w02)], wv.at[1], ws.at[1])
    start_all(got_wa, got_wb)
    stencil_pads(b0, b1)

    def first(r, v, a):
        value = v + 16 * H * a + ra(r)
        ca[r : r + TILE, :] = value
        return value

    def second(r, v, a):
        cb[r : r + TILE, :] = v + 16 * H * a + rb(r)

    run_steps(
        x, (b0, b1), held, [(ready([got_wa]), wv.at[0], first), (ready([got_wb]), wv.at[1], second)]
    )


def relay(name, *args):
    return kernel_call(
        relay_body, (STATE, STATE), (VMEM, VMEM), args, [VMEM] * 4 + [ANY] * 4 + [VMEM] * 2, [*SCRATCH, *wbuf(2)], 2,
        name, 16,
    )


def choose_body(ends, made, got, cb1, cb2, out, sem):
    _, x, z, _ = spot()
    load = Load([((x == 0) & (z < 2), ends), ((x == 0) & (z == 2), made), ((x == 0) & (z == 3), got),
                 (x == 1, cb1), (x >= 2, cb2)], out, sem)
    load.start()
    load.wait()


def choose(*args):
    return kernel_call(choose_body, STATE, VMEM, args, [ANY] * 5, [pltpu.SemaphoreType.DMA], 0, CHOOSE, 8)


def correct_body(first, ends_in, even_in, even2_in, ca1, ca2, came, rhs2, rhs3, we2, we3, wa0, wb0, wa1, wb1,
                 fa0, fb0, fa1, fb1, made, got3, got1, ends, send, move, coarse, b0, b1, held, xv, xs, wv, ws):
    d, xc, z, _ = spot()
    is_a = z % 2 == 0
    is_b = z % 2 == 1
    odd = z >= 2
    third = z == 3
    other = z != 3
    late = (xc == 3) & odd
    x, ra, g0, g1, rk = (xv.at[n] for n in range(5))
    got_x = Load(
        [((xc == 0) & (z < 2), first), ((xc == 0) & (z == 2), ends_in),
         (((xc == 0) & third) | ((xc > 0) & (z < 2) & (d != 25)), even_in), (d == 25, even2_in),
         ((xc == 1) & odd, ca1), ((xc == 2) & odd, ca2), (late, came)], x, xs.at[0])
    got_e = Load([(third, we3), (other, we2)], wv.at[0], ws.at[0])
    got_ra = Load([(third, rhs3), (other, rhs2)], ra, xs.at[1])
    got_w0 = Load([(is_a, wa0), (is_b, wb0)], wv.at[1], ws.at[1])
    got_w1 = Load([(is_a, wa1.at[0]), (is_b, wb1)], wv.at[2], ws.at[2])
    got_f0 = Load([(is_a, fa0), (is_b, fb0)], g0, xs.at[2])
    got_f1 = Load([(is_a, fa1), (is_b, fb1)], g1, xs.at[3])
    got_r = Load(
        [(is_a, made), (third, got3), ((z == 1) & (d // 4 > 0), got1), ((z == 1) & (d // 4 == 0), ends)],
        rk, xs.at[4])
    start_all(got_x, got_e, got_ra)
    stencil_pads(b0, b1)
    got_x.wait()
    wait_all(got_e, got_ra)
    start_all(got_w0, got_f0, got_r, got_w1, got_f1)

    @pl.when(late)
    def _():
        def update(r, v, a):
            held[r : r + TILE, :] = v + 16 * H * a + ra[r : r + TILE, :]

        run_steps(rows(x), (b0, b1), held, [(nothing, wv.at[0], update)])
        x[...] = held[...]

    def zero(r, v, a):
        rk_rows = rk[r : r + TILE, :]
        coarse[r : r + TILE, :] = jnp.where(d // 4 < 2, rk_rows, v + 16 * H * a + rk_rows)
        value = v + 4 * H * a + g0[r : r + TILE, :]
        move[r : r + TILE, :] = value
        send[r : r + TILE, :] = v
        stencil_put(b1, r, value)

    run_steps(rows(x), (b0, b1), held, [(ready([got_w0, got_f0, got_r]), wv.at[1], zero)])
    wait_all(got_w1, got_f1)

    @pl.when(is_b)
    def _():
        for r in range(0, ROWS, TILE):
            at = slice(r, r + TILE)
            value = move[at, :] + 4 * H * relu_conv(b1, wv.at[2], r) + g1[at, :]
            move[at, :] = value
            send[at, :] = value


def correct(*args):
    return kernel_call(
        correct_body, (STATE,) * 3, (VMEM,) * 3, args, [ANY] * 13 + [HBM] + [ANY] * 9,
        [*SCRATCH, *room(5), *wbuf(3)], 3, CORRECT, 22
    )


def second_body(x, w2, f2, out, b0, b1, held, wv, ws):
    _, _, z, core = spot()

    @pl.when((core == 1) & (z % 2 == 1))
    def _():
        got = plain(w2, wv.at[0], ws.at[0])
        got.start()
        stencil_pads(b0, b1)
        run_steps(rows(x), (b0, b1), held, [(ready([got]), wv.at[0], coarse_last(f2, out))])


def second(x, w2, f2):
    return kernel_call(
        second_body, STATE, VMEM, (x, w2, f2), [VMEM, ANY, VMEM], [*SCRATCH, *wbuf(1)], 1, SECOND, 12
    )


def finish_body(x0, xa, xb, coarse, w, rhs, out, b0, b1, held, wv, ws, stage, os):
    _, _, z, core = spot()
    is_b = z % 2 == 1
    last = (core == 1) & is_b
    ww = [plain(w.at[n], wv.at[n], ws.at[n]) for n in range(3)]
    start_all(*ww)
    stencil_pads(b0, b1)

    @pl.loop(0, ROWS // TILE)
    def _(i):
        r = pl.multiple_of(i * TILE, TILE)
        at = pl.ds(r, TILE)
        value = jnp.where(core == 0, x0[at, :], jnp.where(is_b, xb[at, :], xa[at, :]))
        held[at, :] = value
        stencil_put(b0, r, value)

    ww[0].wait()
    for r in range(0, ROWS, TILE):
        at = slice(r, r + TILE)
        a = relu_conv(b0, wv.at[0], r)
        v = held[at, :]
        stage[3, at, :] = jnp.where(last, coarse[at, :], v + 4 * H * a + rhs[at, :])
        value = v + H * a
        stage[0, at, :] = value
        stencil_put(b1, r, value)
    pltpu.make_async_copy(stage.at[0], out.at[0], os.at[0]).start()
    pltpu.make_async_copy(stage.at[3], out.at[3], os.at[3]).start()
    for n, source, target in ((1, b1, b0), (2, b0, b1)):
        ww[n].wait()
        for r in range(0, ROWS, TILE):
            at = slice(r, r + TILE)
            value = stage[n - 1, at, :] + H * relu_conv(source, wv.at[n], r)
            stage[n, at, :] = value
            if n == 1:
                stencil_put(target, r, value)
        pltpu.make_async_copy(stage.at[n], out.at[n], os.at[n]).start()
    for n in range(4):
        pltpu.make_async_copy(stage.at[n], out.at[n], os.at[n]).wait()


OUT = jax.ShapeDtypeStruct((4, ROWS, CH), jnp.float32)


def finish(*args):
    return kernel_call(
        finish_body, OUT, ANY, args, [VMEM] * 4 + [HBM, VMEM],
        [*SCRATCH, *wbuf(3), pltpu.VMEM((4, ROWS, CH), jnp.float32), pltpu.SemaphoreType.DMA((4,))], 3, FINISH, 22,
    )


def widen_body(w, out, wv, sem):
    load = plain(w.at[0], wv, sem)
    load.start()
    load.wait()

    @pl.loop(0, TAPS // TILE)
    def _(n):
        at = pl.ds(pl.multiple_of(n * TILE, TILE), TILE)
        out[at, :] = wv[at, :].astype(jnp.float32)


def widen(w):
    return kernel_call(
        widen_body, jax.ShapeDtypeStruct((TAPS, CH), jnp.float32), VMEM, (w,), [HBM],
        [pltpu.VMEM((TAPS, CH), jnp.bfloat16), pltpu.SemaphoreType.DMA], 0, WIDEN, 8,
    )


def norm_sum_body(a, b, out):
    out[...] = a[...] + b[...]


def norm_sum(a, b):
    return kernel_call(
        norm_sum_body, jax.ShapeDtypeStruct((8, CH), jnp.float32), VMEM, (a, b), [VMEM, VMEM], [], 0, NORM_SUM, 2
    )


def norm_root_body(a, b, out):
    total = jnp.sum(a[...] + b[...])
    root = jnp.sqrt(jnp.full((8, 128), total, jnp.float32) / (4 * ROWS * CH) + 1e-06)
    out[0] = jnp.max(root)


def norm_root(a, b):
    return kernel_call(
        norm_root_body, jax.ShapeDtypeStruct((1,), jnp.float32), pl.BlockSpec(memory_space=pltpu.SMEM), (a, b),
        [VMEM, VMEM], [], 0, NORM_ROOT, 2,
    )


def narrow_body(x, out):
    @pl.loop(0, TAPS // TILE)
    def _(n):
        at = pl.ds(pl.multiple_of(n * TILE, TILE), TILE)
        out[at, :] = x[at, :].astype(jnp.bfloat16)


def narrow(x, name):
    return kernel_call(
        narrow_body, jax.ShapeDtypeStruct((TAPS, CH), jnp.bfloat16), VMEM, (x,), [VMEM], [], 0, name, 8
    )


PART = TAPS // 4


def pack_body(chip, own, narrowed, out):
    start = lax.axis_index("batch") * PART

    @pl.loop(0, TAPS // TILE)
    def _(n):
        at = pl.ds(pl.multiple_of(n * TILE, TILE), TILE)
        narrowed[at, :] = chip[at, :].astype(jnp.bfloat16)

    @pl.loop(0, PART // 64)
    def _(n):
        at = pl.ds(pl.multiple_of(start + n * 64, 64), 64)
        out[pl.ds(pl.multiple_of(n * 64, 64), 64), :] = chip[at, :]
        out[pl.ds(pl.multiple_of(PART + n * 64, 64), 64), :] = own[at, :]


def pack(chip, own):
    return kernel_call(
        pack_body, (jax.ShapeDtypeStruct((TAPS, CH), jnp.bfloat16), jax.ShapeDtypeStruct((2 * PART, CH), jnp.float32)),
        (VMEM, VMEM), (chip, own), [VMEM, VMEM], [], 0, PACK, 8,
    )


def unpack_body(p0, p1, p2, p3, out0, out1):
    y = lax.axis_index("batch")
    for n, part in enumerate((p0, p1, p2, p3)):
        start = (y + 4 - n) % 4 * PART

        @pl.loop(0, PART // 64)
        def _(i, part=part, start=start):
            at = pl.ds(pl.multiple_of(start + i * 64, 64), 64)
            out0[at, :] = part[pl.ds(pl.multiple_of(i * 64, 64), 64), :].astype(jnp.bfloat16)
            out1[at, :] = part[pl.ds(pl.multiple_of(PART + i * 64, 64), 64), :].astype(jnp.bfloat16)


def unpack(*parts):
    kernel = jax.ShapeDtypeStruct((TAPS, CH), jnp.bfloat16)
    return kernel_call(unpack_body, (kernel, kernel), (VMEM, VMEM), parts, [VMEM] * 4, [], 0, UNPACK, 10)


def send(value, pairs, axis="layer"):
    return lax.ppermute(value, axis, pairs)


A0 = [4 * k for k in range(8)]


def cycle(first_state, guess_points, weights):
    first = first_state.reshape(ROWS, CH)
    guess = guess_points.reshape(ROWS, CH)
    w = weights.reshape(4, TAPS, CH)
    shift = [(i, i + 1) for i in range(31)]

    came = send(guess, shift)
    wide = widen(w)
    w_chip = send(wide, [p for k in A0 for p in ((k, k + 1), (k + 2, k + 3))])
    w_z2 = send(wide, [(k + 2, k + 1) for k in A0])
    wn_chip, packed = pack(w_chip, wide)
    part0 = send(packed, [(k + 1, k + 3) for k in A0])
    relaxed = sweep(first, came, w)

    came = send(relaxed, shift)
    w_z3 = send(wide, [(k + 3, k + 1) for k in A0] + [(8 * x, 8 * x + 7) for x in range(1, 4)])
    fine, out0, squares = resweep(first, came, w, relaxed)

    in0 = send(out0, [p for k in A0 for p in ((k, k + 1), (k + 2, k + 3))])
    q1 = one_coarse(in0, w, fine)
    came = send(q1, [(k + 1, k + 3) for k in A0])
    fine_3 = send(fine, [p for k in A0 for p in ((k + 3, k + 1), (k + 1, k + 3))])
    fine_a0 = send(fine, [(k, k + 1) for k in A0])
    ends = two_coarse(came, wn_chip, w, in0, fine)

    ends_in = send(ends, [(k + 3, k + 5) for k in A0[:-1]])
    fine_2 = send(fine, [p for k in A0 for p in ((k + 2, k + 1), (k, k + 3))])
    parts = [part0]
    for n in (1, 2, 3):
        ring = [((k + 3) * 4 + y, (k + 3) * 4 + (y + n) % 4) for k in A0 for y in range(4)]
        parts.append(send(part0, ring, ("layer", "batch")))
    wn_z2, wn_z3 = narrow(w_z2, NARROW_2), narrow(w_z3, NARROW_3)
    w_even2 = send(w_z3, [(8 * x + 7, 8 * x + 5) for x in range(1, 4)])
    made = group(first, ends_in, wn_chip, w, wn_z2, wn_z3, fine_a0, fine, fine_2, fine_3)

    in_c = send(made, [(9, 13), (17, 21), (25, 29), (5, 7), (13, 15), (21, 23), (29, 31)])
    in_a = send(made, [(5, 13), (9, 15), (17, 23), (25, 31)])
    in_d = send(made, [(5, 15), (1, 3), (9, 11), (17, 19), (25, 27)])
    wn_even2 = narrow(w_even2, NARROW_E)
    wn_b0, wn_b1 = unpack(*parts)

    common = (in_c, in_a, wn_even2, wn_z3, wn_chip, wn_b0, made, in_c)
    ca1, cb1 = relay(RELAY1, in_a, in_d, *common)
    came = send(cb1, [(13, 21), (15, 23)])
    swapped = send(squares, [(0, 1), (1, 0), (2, 3), (3, 2)], "batch")
    squares = norm_sum(squares, swapped)
    swapped = send(squares, [(0, 2), (2, 0), (1, 3), (3, 1)], "batch")
    norms = norm_root(squares, swapped)
    ca2, cb2 = relay(RELAY2, came, came, *common)
    came = send(cb2, [(21, 29), (23, 31)])
    carry = choose(ends, made, in_c, cb1, cb2)
    even_in = send(carry, [(3, 7), (5, 11), (7, 9), (13, 19), (15, 17), (21, 27)])
    even2_in = send(came, [(29, 25)])
    out1, move, coarse = correct(
        first, ends_in, even_in, even2_in, ca1, ca2, came, in_c, in_a, wn_even2, wn_z3, wn_chip, wn_b0, w, wn_b1,
        fine_a0, fine_2, fine, fine_3, made, in_c, in_d, ends,
    )
    in1 = send(out1, [p for k in A0 for p in ((k + 1, k), (k + 3, k + 2))])
    moved = second(move, wn_chip, in0)
    states = finish(in1, move, moved, coarse, w, fine)
    return states.reshape(4, 1, SIDE, SIDE, CH), norms


def solution(mesh):
    placed = (
        P("batch", None, None, None),
        P("layer", "batch", None, None, None),
        P("layer", None, None, None, None),
    )
    return jax.shard_map(
        cycle,
        mesh=mesh,
        in_specs=placed,
        out_specs=(P("layer", "batch", None, None, None), P("layer")),
        check_vma=False,
    )
```
